256 devices in a mesh: group: 16 (over x_lo, y, core), dp: 16 (over x_hi, z).
Axes of the slice: x: 4 (x_hi: 2, x_lo: 2; x = x_hi * 2 + x_lo), y: 4, z: 8, core: 2. Of those that a mesh axis runs over, the one named last changes fastest.
Arguments:
- latents: bfloat16 [16, 512, 6144], P('group', 'dp'), may hold values from -6 to 6
- steps: int32 [16], P('group'), may hold values from 0 to 15
- segment_ids: int32 [512], replicated, may hold values from 0 to 15, never falling along the last dimension, each value on 1 to 64 neighbouring positions
- mod_table: float32 [16, 2, 6144], replicated, may hold values from -3 to 3
- w_query: bfloat16 [6144, 4096], P(None, 'dp')
- w_key: bfloat16 [6144, 4096], P(None, 'dp')
- w_value: bfloat16 [6144, 4096], P(None, 'dp'), may hold values from -0.3125 to 0.3125
Outputs:
- attended: bfloat16 [16, 512, 4096], P('group', 'dp')
The draws below stay inside these ranges and needn't reach their ends.
Inputs may be any that keep to these rules, and one draw needn't show every extreme that they name: `segment_ids`: rows of one clip are contiguous; every clip index occurs, a clip holds 1 to 64 rows and one holds exactly that many.
All inputs are finite; a program needn't handle non-finite values.
Results may differ from the reference program's by a relative error of at most 0.011.
Values may be sent and summed in bfloat16 or wider, within the bound.
A program may use at most 128 MiB of HBM per device.

```python
import math
import jax
import jax.numpy as jnp
import numpy as np
from jax import lax

D = 6144
HD = 128
STEPS = 16
ROWS = 32
HEADS = 32
TOKC = 512
GROUPS = 16
N_DP = 16


def shared_keys(key):
    return jax.random.normal(jax.random.fold_in(key, 11), (D, HEADS * HD), jnp.float32) / jnp.sqrt(jnp.float32(D))


def draw_w_key(key, part):
    return shared_keys(key).astype(jnp.bfloat16)


def draw_w_query(key, part):
    fresh = jax.random.normal(jax.random.fold_in(key, 12), (D, HEADS * HD), jnp.float32) * (2.0 / jnp.sqrt(jnp.float32(D)))
    return fresh.astype(jnp.bfloat16)


def set_ends(array, stream_key, low, high):
    spot = [jax.random.randint(jax.random.fold_in(stream_key, axis), (), 0, length) for axis, length in enumerate(array.shape)]
    widest = array.shape.index(max(array.shape))
    beside = spot[:widest] + [(spot[widest] + 1) % array.shape[widest]] + spot[widest + 1:]
    return array.at[tuple(spot)].set(low).at[tuple(beside)].set(high)


def levels(key, extent, pieces, low, high):
    gain = 1.0
    for position, shards_of in pieces:
        draws = jax.random.uniform(jax.random.fold_in(jax.random.fold_in(key, 6), position), (shards_of,), jnp.float32, low / len(pieces), high / len(pieces))
        gain = gain * jnp.repeat(jnp.exp(draws), extent[position] // shards_of).reshape((-1,) + (1,) * (len(extent) - 1 - position))
    return gain


def length_profile(amount, total, most, lean):
    loads = [(1 << 20) // math.isqrt(standing ** lean) + 1 for standing in range(2, amount + 1)]
    surplus, given = total - most - (amount - 1), [1] * (amount - 1)
    while surplus > 0:
        movable = [i for i in range(amount - 1) if given[i] < most]
        whole, left = sum([loads[i] for i in movable]), surplus
        for i in movable:
            extra = min(most - given[i], max(1, left * loads[i] // whole), surplus)
            given[i] = given[i] + extra
            surplus = surplus - extra
    return np.array([most] + given)


def uneven_parts(stream_key, number_of, total, bound, skew):
    if number_of == 2:
        one = jax.random.randint(stream_key, (), max(1, total - bound), min(bound, total - 1) + 1)
        return jnp.stack([one, total - one])
    tallies = jnp.asarray(length_profile(number_of, total, bound, skew), jnp.int32)
    pairs = (number_of - 1) // 2
    giver, taker = tallies[1:1 + 2 * pairs:2], tallies[2:2 + 2 * pairs:2]
    slack = jnp.minimum(giver - 1, bound - taker)
    passed = jax.random.randint(jax.random.fold_in(stream_key, 1), (pairs,), 0, 1 << 20) % (slack + 1)
    tallies = tallies.at[1:1 + 2 * pairs:2].set(giver - passed).at[2:2 + 2 * pairs:2].set(taker + passed)
    return tallies[jax.random.permutation(jax.random.fold_in(stream_key, 2), number_of)]


def noise(stream_key, dims, width, bound, split=(), kind=jnp.bfloat16):
    loudness = levels(stream_key, dims, split, -0.22, 0.18) if split else 1.0
    values = jax.random.normal(stream_key, dims, jnp.float32) * width * loudness
    return jnp.minimum(jnp.maximum(values, -bound), bound).astype(kind)


def setup_inputs(seed: int = 0) -> dict:
    key_list = jax.random.split(jax.random.key(seed), 8)
    latents = noise(key_list[0], (GROUPS, TOKC, D), 1.0, 6.0, ((0, 16), (1, 16)))
    steps = set_ends(jax.random.randint(key_list[1], (GROUPS,), 0, STEPS), jax.random.fold_in(key_list[1], 1), 0, STEPS - 1).astype(jnp.int32)
    segment_ids = jnp.searchsorted(jnp.cumsum(uneven_parts(key_list[2], N_DP, TOKC, 2 * ROWS, 2)), jnp.arange(TOKC), side="right").astype(jnp.int32)
    mod_table = noise(key_list[3], (STEPS, 2, D), 0.5, 3.0, (), jnp.float32)
    w_query = draw_w_query(jax.random.fold_in(key_list[7], 71), 0)
    w_key = draw_w_key(jax.random.fold_in(key_list[7], 71), 0)
    w_value = noise(key_list[6], (D, HEADS * HD), (D // 16) ** -0.5, 0.3125, ((1, 16),))
    return dict(latents=latents, steps=steps, segment_ids=segment_ids, mod_table=mod_table, w_query=w_query, w_key=w_key, w_value=w_value)


def reference(latents, steps, segment_ids, mod_table, w_query, w_key, w_value):
    groups = latents.shape[0]
    tokc = latents.shape[1]
    x = latents.astype(jnp.float32)
    normed = x * lax.rsqrt(lax.optimization_barrier(jnp.mean(x * x, axis=-1, keepdims=True)) + 1e-06)
    picker = (steps[:, None] == jnp.arange(STEPS, dtype=jnp.int32)[None, :]).astype(jnp.float32)
    modulation = jnp.dot(picker, mod_table.reshape(STEPS, 2 * D), precision=lax.Precision.HIGHEST)
    rows = (normed * (1.0 + modulation[:, None, :D]) + modulation[:, None, D:]).astype(jnp.bfloat16)
    rows = rows.reshape(groups * tokc, D)
    query = jnp.dot(rows, w_query, preferred_element_type=jnp.float32).astype(jnp.bfloat16).reshape(groups, tokc, HEADS, HD)
    keys = jnp.dot(rows, w_key, preferred_element_type=jnp.float32).astype(jnp.bfloat16).reshape(groups, tokc, HEADS, HD)
    values = jnp.dot(rows, w_value, preferred_element_type=jnp.float32).astype(jnp.bfloat16).reshape(groups, tokc, HEADS, HD)
    same_clip = segment_ids[:, None] == segment_ids[None, :]
    inverse = 1.0 / math.sqrt(HD)
    outputs = []
    for group in range(groups):
        key_rows = keys[:group + 1].reshape((group + 1) * tokc, HEADS, HD).astype(jnp.float32)
        value_rows = values[:group + 1].reshape((group + 1) * tokc, HEADS, HD).astype(jnp.float32)
        allowed = jnp.tile(same_clip, (1, group + 1))
        scores = jnp.einsum('thd,khd->htk', query[group].astype(jnp.float32), key_rows) * inverse
        scores = jnp.where(allowed[None], scores, -1e+30)
        highest = lax.optimization_barrier(jnp.max(scores, axis=-1, keepdims=True))
        weights = jnp.where(allowed[None], jnp.exp(scores - highest), 0.0)
        total = lax.optimization_barrier(jnp.sum(weights, axis=-1))
        rounded = lax.optimization_barrier(weights.astype(jnp.bfloat16))
        summed = jnp.einsum('htk,khd->thd', rounded.astype(jnp.float32), value_rows)
        result = summed / jnp.transpose(total)[:, :, None]
        outputs.append(result.reshape(tokc, HEADS * HD).astype(jnp.bfloat16))
    return jnp.stack(outputs)
```

```python
import math

import jax
import jax.numpy as jnp
from jax import lax
from jax.experimental import pallas as pl
from jax.experimental.pallas import tpu as pltpu
from jax.sharding import PartitionSpec as P

D = 6144
HD = 128
HALF = D // 2
MESH = pl.DeviceIdType.MESH
NEG = -1e30
BF = jnp.bfloat16
F32 = jnp.float32


def kernel(
    lat, steps, seg, mod, wq, wk, wv, out,
    x_buf, w_buf, mod_all, mod_row, xn, q_own, kv_own, q_in, kv_in, s_buf, bias, seg_buf, o_buf, o_in,
    xs, xr, ls, es, er, os_, or_,
):
    g = lax.axis_index("group")
    d = lax.axis_index("dp")
    xh = d // 8
    z = d % 8
    head = g // 8
    win = g % 8

    def at_z(k):
        return {"group": g, "dp": xh * 8 + (z + k + 8) % 8}

    across = {"group": g, "dp": (d + 8) % 16}
    up, down = at_z(1), at_z(-1)

    barrier = pltpu.get_barrier_semaphore()
    for peer in (up, down, across):
        pl.semaphore_signal(barrier, inc=1, device_id=peer, device_id_type=MESH)
    for k in range(1, 16):
        pl.semaphore_signal(barrier, inc=1, device_id={"group": (g + k) % 16, "dp": d}, device_id_type=MESH)

    def own_slot(half):
        return 2 * d + half

    def other(k, half):
        return 2 * ((1 - xh) * 8 + (z + k + 8) % 8) + half

    def same(k, half):
        return 2 * (xh * 8 + (z + k + 8) % 8) + half

    loads = [
        pltpu.make_async_copy(lat.at[0, pl.ds(0, 16)], x_buf.at[own_slot(0)], ls.at[0]),
        pltpu.make_async_copy(lat.at[0, pl.ds(16, 16)], x_buf.at[own_slot(1)], ls.at[1]),
        pltpu.make_async_copy(mod, mod_all, ls.at[2]),
        pltpu.make_async_copy(seg, seg_buf, ls.at[3]),
        pltpu.make_async_copy(wq, w_buf.at[0], ls.at[4]),
        pltpu.make_async_copy(wk, w_buf.at[1], ls.at[5]),
        pltpu.make_async_copy(wv, w_buf.at[2], ls.at[6]),
    ]
    for c in loads:
        c.start()
    pl.semaphore_wait(barrier, 18)

    sends = []

    def send(src, dst, to, recv):
        c = pltpu.make_async_remote_copy(
            src_ref=src, dst_ref=dst, send_sem=xs.at[len(sends)], recv_sem=recv, device_id=to, device_id_type=MESH
        )
        c.start()
        sends.append(c)

    def send_own(half, to):
        send(lat.at[0, pl.ds(16 * half, 16)], x_buf.at[own_slot(half)], to, xr.at[own_slot(half)])

    def relay(slot, to):
        send(x_buf.at[slot], x_buf.at[slot], to, xr.at[slot])

    def relay_half(slot, part, to):
        cols = pl.ds(part * HALF, HALF)
        sem = xr.at[slot] if part == 0 else xr.at[32]
        send(x_buf.at[slot, :, cols], x_buf.at[slot, :, cols], to, sem)

    def arrived(slot):
        pltpu.make_async_remote_copy(
            src_ref=x_buf.at[slot], dst_ref=x_buf.at[slot], send_sem=xs.at[0], recv_sem=xr.at[slot],
            device_id=up, device_id_type=MESH,
        ).wait_recv()

    def arrived_half(slot, part):
        cols = pl.ds(part * HALF, HALF)
        sem = xr.at[slot] if part == 0 else xr.at[32]
        pltpu.make_async_remote_copy(
            src_ref=x_buf.at[slot, :, cols], dst_ref=x_buf.at[slot, :, cols], send_sem=xs.at[0], recv_sem=sem,
            device_id=up, device_id_type=MESH,
        ).wait_recv()

    send_own(0, up)
    send_own(0, down)
    send_own(0, across)
    send_own(1, up)
    send_own(1, down)
    send_own(1, across)

    loads[2].wait()
    row = mod_all[steps[0]]
    mod_row[0:1, :] = 1.0 + row[0:1, :]
    mod_row[1:2, :] = row[1:2, :]
    loads[3].wait()
    for w in range(8):
        first = min(max(64 * w - 64, 0), 320)

        @pl.when(win == w)
        def _(w=w, first=first):
            sq = jnp.broadcast_to(seg_buf[0:1, 64 * w : 64 * w + 64], (64, 64))
            diag = lax.broadcasted_iota(jnp.int32, (64, 64), 0) == lax.broadcasted_iota(jnp.int32, (64, 64), 1)
            col = jnp.sum(jnp.where(diag, sq, 0.0), axis=1, keepdims=True)
            sk = seg_buf[0:1, first : first + 192]
            tile = jnp.where(col == sk, 0.0, NEG)
            wide = jnp.concatenate([tile] * 4, axis=1)
            for i in range(4):
                bias[0, 64 * i : 64 * i + 64, :] = wide
                parts = [tile if j <= i else jnp.full((64, 192), NEG, F32) for j in range(4)]
                bias[1, 64 * i : 64 * i + 64, :] = jnp.concatenate(parts, axis=1)

    def norm(slot, at):
        x = x_buf[slot].astype(F32)
        inv = lax.rsqrt(jnp.mean(x * x, axis=-1, keepdims=True) + 1e-06)
        xn[pl.ds(16 * at, 16), :] = (x * inv * mod_row[0:1, :] + mod_row[1:2, :]).astype(BF)

    def project(which, slots):
        n = 16 * len(slots)
        r = jnp.dot(xn[0:n, :], w_buf[which], preferred_element_type=F32).astype(BF)
        for i, slot in enumerate(slots):
            for h in range(2):
                piece = r[16 * i : 16 * i + 16, HD * h : HD * h + HD]
                if which == 0:
                    q_own[h, slot] = piece
                else:
                    kv_own[h, slot, :, HD * (which - 1) : HD * which] = piece

    loads[0].wait()
    loads[1].wait()
    norm(own_slot(0), 0)
    norm(own_slot(1), 1)

    arrived(other(0, 0))
    relay(other(0, 0), up)
    relay(other(0, 0), down)
    chunk = [own_slot(0), own_slot(1), other(0, 0), other(0, 1)]

    for s in range(1, 4):
        a, b = same(-s, 0), same(s, 0)
        arrived(a)
        relay(a, up)
        arrived(b)
        if s < 3:
            relay(b, down)
        if s == 1:
            norm(chunk[2], 2)
        else:
            for i in range(4):
                norm(chunk[i], i)
        a, b = same(-s, 1), same(s, 1)
        arrived(a)
        if s < 3:
            relay(a, up)
        relay(a, across)
        arrived(b)
        relay(b, down)
        relay(b, across)
        if s == 1:
            arrived(chunk[3])
            norm(chunk[3], 3)
            for i in (4, 5, 6):
                loads[i].wait()
        else:
            norm(chunk[4], 4)
            norm(chunk[5], 5)
        a, b = other(-s, 0), other(s, 0)
        arrived(a)
        if s < 3:
            relay(a, up)
        else:
            relay_half(a, 0, up)
        arrived(b)
        if s < 3:
            relay(b, down)
        else:
            relay_half(b, 1, down)
        if s > 1:
            for i in (6, 7):
                arrived(chunk[i])
                norm(chunk[i], i)
        for which in range(3):
            project(which, chunk)
        chunk = [same(-s, 0), same(s, 0), same(-s, 1), same(s, 1), other(-s, 0), other(s, 0), other(-s, 1), other(s, 1)]

    for i in range(4):
        norm(chunk[i], i)
    arrived(same(4, 1))
    relay(same(4, 1), across)
    arrived(same(4, 0))
    norm(chunk[4], 4)
    norm(chunk[5], 5)
    for i in (6, 7):
        arrived(chunk[i])
        norm(chunk[i], i)
    for which in range(3):
        project(which, chunk)
    chunk = [same(4, 0), same(4, 1), other(4, 0), other(4, 1)]
    norm(chunk[0], 0)
    norm(chunk[1], 1)
    arrived_half(chunk[2], 0)
    arrived_half(chunk[2], 1)
    norm(chunk[2], 2)
    arrived(chunk[3])
    norm(chunk[3], 3)
    for which in range(3):
        project(which, chunk)

    ex = []
    for k in range(1, 16):
        t = (g + k) % 16
        th, tw = t // 8, t % 8
        first = jnp.minimum(jnp.maximum(4 * tw - 4, 0), 20)
        to = {"group": t, "dp": d}
        ex.append(
            pltpu.make_async_remote_copy(
                src_ref=kv_own.at[th, pl.ds(first, 12)], dst_ref=kv_in.at[g], send_sem=es.at[0, k],
                recv_sem=er.at[0, g], device_id=to, device_id_type=MESH,
            )
        )
        ex.append(
            pltpu.make_async_remote_copy(
                src_ref=q_own.at[th, pl.ds(4 * tw, 4)], dst_ref=q_in.at[g], send_sem=es.at[1, k],
                recv_sem=er.at[1, g], device_id=to, device_id_type=MESH,
            )
        )
    for c in ex:
        c.start()
    first = jnp.minimum(jnp.maximum(4 * win - 4, 0), 20)
    mine = [
        pltpu.make_async_copy(kv_own.at[head, pl.ds(first, 12)], kv_in.at[g], ls.at[7]),
        pltpu.make_async_copy(q_own.at[head, pl.ds(4 * win, 4)], q_in.at[g], ls.at[8]),
    ]
    for c in mine:
        c.start()
    for c in mine:
        c.wait()
    for k in range(1, 16):
        t = (g + k) % 16
        for i, (own, land) in enumerate(((kv_own.at[0, pl.ds(0, 12)], kv_in.at[t]), (q_own.at[0, pl.ds(0, 4)], q_in.at[t]))):
            pltpu.make_async_remote_copy(
                src_ref=own, dst_ref=land, send_sem=es.at[i, k], recv_sem=er.at[i, t], device_id=up, device_id_type=MESH
            ).wait_recv()

    scale = 1.0 / math.sqrt(HD)
    outs = []
    for b in range(4):
        q = q_in[4 * b : 4 * b + 4].reshape(256, HD)
        best = jnp.full((256, 1), NEG, F32)
        for kb in range(b + 1):
            keys = kv_in[4 * kb : 4 * kb + 4, :, :, 0:HD].reshape(768, HD)
            sc = lax.dot_general(q, keys, (((1,), (1,)), ((), ())), preferred_element_type=F32)
            sc = sc * scale + bias[1 if kb == b else 0]
            s_buf[:, 768 * kb : 768 * kb + 768] = sc
            best = jnp.maximum(best, jnp.max(sc, axis=-1, keepdims=True))
        total = jnp.zeros((256, 1), F32)
        acc = jnp.zeros((256, HD), F32)
        for kb in range(b + 1):
            p = jnp.exp(s_buf[:, 768 * kb : 768 * kb + 768] - best)
            total = total + jnp.sum(p, axis=-1, keepdims=True)
            vals = kv_in[4 * kb : 4 * kb + 4, :, :, HD : 2 * HD].reshape(768, HD)
            acc = acc + jnp.dot(p.astype(BF), vals, preferred_element_type=F32)
        o_buf[4 * b : 4 * b + 4] = (acc / total).astype(BF).reshape(4, 4, 16, HD)

    col = pl.multiple_of((2 * d + head) * HD, HD)
    cols = pl.ds(col, HD)
    for half in range(2):
        td = 2 * win + half
        for c in range(16):
            src = o_buf.at[c, pl.ds(2 * half, 2)]
            dst = o_in.at[:, :, cols]
            away = jnp.logical_or(g != c, d != td)
            rc = pltpu.make_async_remote_copy(
                src_ref=src, dst_ref=dst, send_sem=os_.at[half, c], recv_sem=or_.at[2 * d + head],
                device_id={"group": c, "dp": td}, device_id_type=MESH,
            )
            lc = pltpu.make_async_copy(src, dst, ls.at[9])

            @pl.when(away)
            def _(rc=rc):
                rc.start()

            @pl.when(jnp.logical_not(away))
            def _(lc=lc):
                lc.start()
                lc.wait()

    for hd in range(32):
        src_g = (hd % 2) * 8 + d // 2
        here = jnp.logical_and(src_g == g, hd // 2 == d)

        @pl.when(jnp.logical_not(here))
        def _(hd=hd):
            pltpu.make_async_remote_copy(
                src_ref=o_buf.at[0, pl.ds(0, 2)], dst_ref=o_in.at[:, :, pl.ds(hd * HD, HD)], send_sem=os_.at[0, 0],
                recv_sem=or_.at[hd], device_id=up, device_id_type=MESH,
            ).wait_recv()

    final = pltpu.make_async_copy(o_in, out, ls.at[10])
    final.start()

    for c in sends:
        c.wait_send()
    for c in ex:
        c.wait_send()
    for half in range(2):
        td = 2 * win + half
        for c in range(16):
            away = jnp.logical_or(g != c, d != td)

            @pl.when(away)
            def _(half=half, c=c):
                pltpu.make_async_remote_copy(
                    src_ref=o_buf.at[c, pl.ds(2 * half, 2)], dst_ref=o_in.at[:, :, pl.ds(0, HD)], send_sem=os_.at[half, c],
                    recv_sem=or_.at[0], device_id=up, device_id_type=MESH,
                ).wait_send()
    final.wait()


def per_device(latents, steps, segment_ids, mod_table, w_query, w_key, w_value):
    anywhere = pl.BlockSpec(memory_space=pl.ANY)
    vmem = pltpu.VMEM
    dma = pltpu.SemaphoreType.DMA
    out = pl.pallas_call(
        kernel,
        out_shape=jax.ShapeDtypeStruct((2, 16, 4096), BF),
        in_specs=[anywhere, pl.BlockSpec(memory_space=pltpu.SMEM)] + [anywhere] * 5,
        out_specs=anywhere,
        scratch_shapes=[
            vmem((32, 16, D), BF),
            vmem((3, D, 256), BF),
            vmem((16, 2, D), F32),
            vmem((2, D), F32),
            vmem((128, D), BF),
            vmem((2, 32, 16, HD), BF),
            vmem((2, 32, 16, 2 * HD), BF),
            vmem((16, 4, 16, HD), BF),
            vmem((16, 12, 16, 2 * HD), BF),
            vmem((256, 3072), F32),
            vmem((2, 256, 768), F32),
            vmem((1, 512), F32),
            vmem((16, 4, 16, HD), BF),
            vmem((2, 16, 4096), BF),
            dma((48,)),
            dma((33,)),
            dma((11,)),
            dma((2, 16)),
            dma((2, 16)),
            dma((2, 16)),
            dma((32,)),
        ],
        name="block",
        compiler_params=pltpu.CompilerParams(
            collective_id=0, has_side_effects=True, vmem_limit_bytes=58 * 1024 * 1024
        ),
    )(latents, steps, segment_ids.astype(F32).reshape(1, 512), mod_table, w_query, w_key, w_value)
    return out.reshape(1, 32, 4096)


def solution(mesh):
    placed = (
        P("group", "dp", None),
        P("group"),
        P(),
        P(),
        P(None, "dp"),
        P(None, "dp"),
        P(None, "dp"),
    )
    return jax.shard_map(
        per_device, mesh=mesh, in_specs=placed, out_specs=P("group", "dp", None), check_vma=False
    )
```

```python
import math

import jax
import jax.numpy as jnp
from jax import lax
from jax.experimental import pallas as pl
from jax.experimental.pallas import tpu as pltpu
from jax.sharding import PartitionSpec as P

D = 6144
HD = 128
HALF = D // 2
MESH = pl.DeviceIdType.MESH
NEG = -1e30
BF = jnp.bfloat16
F32 = jnp.float32


def kernel(
    lat, steps, seg, mod, wq, wk, wv, out,
    x_buf, w_buf, mod_all, mod_row, xn, own, partner, q_in, kv_in, s_buf, bias, seg_buf, o_buf, o_in,
    xs, xr, ls, ps, pr, es, er, lx, os_, or_,
):
    g = lax.axis_index("group")
    d = lax.axis_index("dp")
    xh = d // 8
    z = d % 8
    head = g // 8
    mate = (g + 8) % 16
    win = (g % 8 + 2 * z) % 8

    def at_z(k):
        return {"group": g, "dp": xh * 8 + (z + k + 8) % 8}

    across = {"group": g, "dp": (d + 8) % 16}
    up, down = at_z(1), at_z(-1)

    barrier = pltpu.get_barrier_semaphore()
    for peer in (up, down, across):
        pl.semaphore_signal(barrier, inc=1, device_id=peer, device_id_type=MESH)
    for k in range(1, 8):
        pl.semaphore_signal(
            barrier, inc=1, device_id={"group": head * 8 + (g + k) % 8, "dp": d}, device_id_type=MESH
        )
    pl.semaphore_signal(barrier, inc=1, device_id={"group": mate, "dp": d}, device_id_type=MESH)

    def block_same(k):
        return xh * 8 + (z + k + 8) % 8

    def block_other(k):
        return (1 - xh) * 8 + (z + k + 8) % 8

    def same(k, half):
        return 2 * block_same(k) + half

    def other(k, half):
        return 2 * block_other(k) + half

    loads = [
        pltpu.make_async_copy(lat.at[0, pl.ds(0, 16)], x_buf.at[same(0, 0)], ls.at[0]),
        pltpu.make_async_copy(lat.at[0, pl.ds(16, 16)], x_buf.at[same(0, 1)], ls.at[1]),
        pltpu.make_async_copy(mod, mod_all, ls.at[2]),
        pltpu.make_async_copy(seg, seg_buf, ls.at[3]),
        pltpu.make_async_copy(wq, w_buf.at[0], ls.at[4]),
        pltpu.make_async_copy(wk, w_buf.at[1], ls.at[5]),
        pltpu.make_async_copy(wv, w_buf.at[2], ls.at[6]),
    ]
    for c in loads:
        c.start()
    pl.semaphore_wait(barrier, 11)

    sends = []

    def send(src, dst, to, recv):
        c = pltpu.make_async_remote_copy(
            src_ref=src, dst_ref=dst, send_sem=xs.at[len(sends)], recv_sem=recv, device_id=to, device_id_type=MESH
        )
        c.start()
        sends.append(c)

    def send_own(half, to):
        send(lat.at[0, pl.ds(16 * half, 16)], x_buf.at[same(0, half)], to, xr.at[same(0, half)])

    def relay(slot, to):
        send(x_buf.at[slot], x_buf.at[slot], to, xr.at[slot])

    def relay_half(slot, part, to):
        cols = pl.ds(part * HALF, HALF)
        sem = xr.at[slot] if part == 0 else xr.at[32]
        send(x_buf.at[slot, :, cols], x_buf.at[slot, :, cols], to, sem)

    def arrived(slot):
        pltpu.make_async_remote_copy(
            src_ref=x_buf.at[slot], dst_ref=x_buf.at[slot], send_sem=xs.at[0], recv_sem=xr.at[slot],
            device_id=up, device_id_type=MESH,
        ).wait_recv()

    def arrived_half(slot, part):
        cols = pl.ds(part * HALF, HALF)
        sem = xr.at[slot] if part == 0 else xr.at[32]
        pltpu.make_async_remote_copy(
            src_ref=x_buf.at[slot, :, cols], dst_ref=x_buf.at[slot, :, cols], send_sem=xs.at[0], recv_sem=sem,
            device_id=up, device_id_type=MESH,
        ).wait_recv()

    send_own(0, across)
    send_own(0, up)
    send_own(0, down)
    send_own(1, up)
    send_own(1, down)
    send_own(1, across)

    loads[2].wait()
    row = mod_all[steps[0]]
    mod_row[0:1, :] = 1.0 + row[0:1, :]
    mod_row[1:2, :] = row[1:2, :]
    loads[3].wait()
    for w in range(8):
        first = min(max(64 * w - 64, 0), 320)

        @pl.when(win == w)
        def _(w=w, first=first):
            sq = jnp.broadcast_to(seg_buf[0:1, 64 * w : 64 * w + 64].astype(F32), (64, 64))
            diag = lax.broadcasted_iota(jnp.int32, (64, 64), 0) == lax.broadcasted_iota(jnp.int32, (64, 64), 1)
            col = jnp.sum(jnp.where(diag, sq, 0.0), axis=1, keepdims=True)
            sk = seg_buf[0:1, first : first + 192].astype(F32)
            tile = jnp.where(col == sk, 0.0, NEG)
            wide = jnp.concatenate([tile] * 4, axis=1)
            for i in range(4):
                bias[0, 64 * i : 64 * i + 64, :] = wide
                parts = [tile if j <= i else jnp.full((64, 192), NEG, F32) for j in range(4)]
                bias[1, 64 * i : 64 * i + 64, :] = jnp.concatenate(parts, axis=1)

    def norm(slot, at):
        x = x_buf[slot].astype(F32)
        inv = lax.rsqrt(jnp.mean(x * x, axis=-1, keepdims=True) + 1e-06)
        xn[pl.ds(16 * at, 16), :] = (x * inv * mod_row[0:1, :] + mod_row[1:2, :]).astype(BF)

    def project(which, slots):
        n = 16 * len(slots)
        r = jnp.dot(xn[0:n, :], w_buf[which], preferred_element_type=F32).astype(BF)
        for i, slot in enumerate(slots):
            for h in range(2):
                own[h, slot, :, HD * which : HD * which + HD] = r[16 * i : 16 * i + 16, HD * h : HD * h + HD]

    def swap(block):
        two = pl.ds(2 * block, 2)
        return pltpu.make_async_remote_copy(
            src_ref=own.at[1 - head, two], dst_ref=partner.at[two], send_sem=ps.at[block], recv_sem=pr.at[block],
            device_id={"group": mate, "dp": d}, device_id_type=MESH,
        )

    def spread(block, whose):
        src = own.at[head] if whose == 0 else partner
        c = g if whose == 0 else mate
        two = pl.ds(2 * block, 2)
        mid = block // 2

        def to_window(i, carry):
            w = mid + i - 2
            cw = jnp.minimum(jnp.maximum(w, 1), 6)
            near = jnp.logical_and(mid - cw <= 1, cw - mid <= 1)
            use = jnp.logical_and(near, jnp.logical_and(w >= 0, w <= 7))
            place = (w + 16 - 2 * z) % 8
            here = place == g % 8
            to = {"group": head * 8 + place, "dp": d}
            rest = pl.ds(2 * block - 4 * (cw - 1), 2)
            kv_src, kv_dst = src.at[two, :, pl.ds(HD, 2 * HD)], kv_in.at[c, rest]
            q_src, q_dst = src.at[two, :, pl.ds(0, HD)], q_in.at[c, pl.ds(2 * (block % 2), 2)]

            @pl.when(jnp.logical_and(use, jnp.logical_not(here)))
            def _():
                pltpu.make_async_remote_copy(
                    src_ref=kv_src, dst_ref=kv_dst, send_sem=es.at[0, whose, place], recv_sem=er.at[0, c],
                    device_id=to, device_id_type=MESH,
                ).start()

            @pl.when(jnp.logical_and(use, here))
            def _():
                pltpu.make_async_copy(kv_src, kv_dst, lx.at[0, whose]).start()

            @pl.when(jnp.logical_and(i == 2, jnp.logical_not(here)))
            def _():
                pltpu.make_async_remote_copy(
                    src_ref=q_src, dst_ref=q_dst, send_sem=es.at[1, whose, place], recv_sem=er.at[1, c],
                    device_id=to, device_id_type=MESH,
                ).start()

            @pl.when(jnp.logical_and(i == 2, here))
            def _():
                pltpu.make_async_copy(q_src, q_dst, lx.at[1, whose]).start()

            return carry

        lax.fori_loop(0, 5, to_window, 0)

    todo = []

    def work(budget):
        while todo and budget > 0:
            cost, call = todo.pop(0)
            call()
            budget -= cost

    def norms(slots, at, wait):
        def call():
            for i in at:
                if wait:
                    arrived(slots[i])
                norm(slots[i], i)
        return call

    def plan(slots, blocks, before):
        n = len(slots)
        for at in range(0, n, 2):
            todo.append((0.5 if at < 4 else 1.0, norms(slots, (at, at + 1), at == 6)))
        for which in range(3):
            todo.append((1.0, lambda which=which: project(which, slots)))

        def out_own():
            for b in blocks:
                swap(b).start()
            for b in blocks:
                spread(b, 0)

        todo.append((1.0, out_own))
        if before:
            todo.append((0.5, lambda: out_mate(before)))

    def out_mate(blocks):
        for b in blocks:
            swap(b).wait_recv()
        for b in blocks:
            spread(b, 1)

    arrived(other(0, 0))
    relay(other(0, 0), up)
    relay(other(0, 0), down)
    loads[0].wait()
    loads[1].wait()
    slots = [same(0, 0), same(0, 1), other(0, 0), other(0, 1)]
    blocks = [block_same(0), block_other(0)]
    todo.append((0.5, norms(slots, (0, 1), False)))
    todo.append((0.5, norms(slots, (2,), False)))

    def ready():
        for i in (4, 5, 6):
            loads[i].wait()
        arrived(slots[3])
        norm(slots[3], 3)

    todo.append((0.5, lambda ready=ready: ready()))
    for which in range(3):
        todo.append((1.0, lambda which=which, slots=slots: project(which, slots)))

    def first_out(blocks=blocks):
        for b in blocks:
            swap(b).start()
        for b in blocks:
            spread(b, 0)

    todo.append((1.0, first_out))

    before = blocks
    for s in range(1, 4):
        for half in range(2):
            a, b = same(-s, half), same(s, half)
            arrived(a)
            if s < 3 or half == 0:
                relay(a, up)
            if half == 1:
                relay(a, across)
            work(1.0)
            arrived(b)
            if s < 3 or half == 1:
                relay(b, down)
            if half == 1:
                relay(b, across)
            work(1.0)
        a, b = other(-s, 0), other(s, 0)
        arrived(a)
        if s < 3:
            relay(a, up)
        else:
            relay_half(a, 0, up)
        work(1.0)
        arrived(b)
        if s < 3:
            relay(b, down)
        else:
            relay_half(b, 1, down)
        work(1.0)
        chunk = [same(-s, 0), same(s, 0), same(-s, 1), same(s, 1), other(-s, 0), other(s, 0), other(-s, 1), other(s, 1)]
        blocks = [block_same(-s), block_same(s), block_other(-s), block_other(s)]
        plan(chunk, blocks, before)
        before = blocks

    work(1.0)
    arrived(same(4, 1))
    relay(same(4, 1), across)
    work(100.0)
    chunk = [same(4, 0), same(4, 1), other(4, 0), other(4, 1)]
    blocks = [block_same(4), block_other(4)]
    arrived(chunk[0])
    norm(chunk[0], 0)
    norm(chunk[1], 1)
    out_mate(before)
    arrived_half(chunk[2], 0)
    arrived_half(chunk[2], 1)
    norm(chunk[2], 2)
    arrived(chunk[3])
    norm(chunk[3], 3)
    for which in range(3):
        project(which, chunk)
    for b in blocks:
        swap(b).start()
    for b in blocks:
        spread(b, 0)
    out_mate(blocks)

    kv_whole, q_whole = own.at[0, pl.ds(0, 12), :, pl.ds(HD, 2 * HD)], own.at[0, pl.ds(0, 4), :, pl.ds(0, HD)]

    def whole(i, whose, place, c):
        return pltpu.make_async_remote_copy(
            src_ref=(kv_whole, q_whole)[i], dst_ref=(kv_in, q_in)[i].at[c], send_sem=es.at[i, whose, place],
            recv_sem=er.at[i, c], device_id=up, device_id_type=MESH,
        )

    for whose in range(2):
        c = (g, mate)[whose]
        pltpu.make_async_copy(kv_whole, kv_in.at[c], lx.at[0, whose]).wait()
        pltpu.make_async_copy(q_whole, q_in.at[c], lx.at[1, whose]).wait()
    for k in range(1, 8):
        c = (g + k) % 8
        for side in range(2):
            for i in range(2):
                whole(i, 0, 0, c + 8 * side).wait_recv()

    scale = 1.0 / math.sqrt(HD)

    def attend(b):
        q = q_in[4 * b : 4 * b + 4].reshape(256, HD)
        best = jnp.full((256, 1), NEG, F32)
        for kb in range(b + 1):
            keys = kv_in[4 * kb : 4 * kb + 4, :, :, 0:HD].reshape(768, HD)
            sc = lax.dot_general(q, keys, (((1,), (1,)), ((), ())), preferred_element_type=F32)
            sc = sc * scale + bias[1 if kb == b else 0]
            s_buf[:, 768 * kb : 768 * kb + 768] = sc
            best = jnp.maximum(best, jnp.max(sc, axis=-1, keepdims=True))
        total = jnp.zeros((256, 1), F32)
        acc = jnp.zeros((256, HD), F32)
        for kb in range(b + 1):
            p = jnp.exp(s_buf[:, 768 * kb : 768 * kb + 768] - best)
            total = total + jnp.sum(p, axis=-1, keepdims=True)
            vals = kv_in[4 * kb : 4 * kb + 4, :, :, HD : 2 * HD].reshape(768, HD)
            acc = acc + jnp.dot(p.astype(BF), vals, preferred_element_type=F32)
        o_buf[4 * b : 4 * b + 4] = (acc / total).astype(BF).reshape(4, 4, 16, HD)

    cols = pl.ds(pl.multiple_of((2 * d + head) * HD, HD), HD)

    def home(c, half):
        return pltpu.make_async_remote_copy(
            src_ref=o_buf.at[c, pl.ds(2 * half, 2)], dst_ref=o_in.at[:, :, cols], send_sem=os_.at[half, c],
            recv_sem=or_.at[2 * d + head], device_id={"group": c, "dp": 2 * win + half}, device_id_type=MESH,
        )

    def away(c, half):
        return jnp.logical_or(g != c, d != 2 * win + half)

    def send_home(b):
        for c in range(4 * b, 4 * b + 4):
            for half in range(2):
                far = away(c, half)

                @pl.when(far)
                def _(c=c, half=half):
                    home(c, half).start()

                @pl.when(jnp.logical_not(far))
                def _(c=c, half=half):
                    lc = pltpu.make_async_copy(o_buf.at[c, pl.ds(2 * half, 2)], o_in.at[:, :, cols], ls.at[7])
                    lc.start()
                    lc.wait()

    attend(3)
    for b in (2, 1, 0):
        attend(b)
        send_home(b + 1)
    send_home(0)

    for hd in range(32):
        src_d = hd // 2
        src_g = (hd % 2) * 8 + (d // 2 + 16 - 2 * (src_d % 8)) % 8
        remote = jnp.logical_or(src_g != g, src_d != d)

        @pl.when(remote)
        def _(hd=hd):
            pltpu.make_async_remote_copy(
                src_ref=o_buf.at[0, pl.ds(0, 2)], dst_ref=o_in.at[:, :, pl.ds(hd * HD, HD)], send_sem=os_.at[0, 0],
                recv_sem=or_.at[hd], device_id=up, device_id_type=MESH,
            ).wait_recv()

    final = pltpu.make_async_copy(o_in, out, ls.at[8])
    final.start()

    for c in sends:
        c.wait_send()
    for b in range(16):
        swap(b).wait_send()
    for k in range(1, 8):
        w = (g + k) % 8
        for whose in range(2):
            for i in range(2):
                whole(i, whose, w, 0).wait_send()
    for half in range(2):
        for c in range(16):
            @pl.when(away(c, half))
            def _(half=half, c=c):
                home(c, half).wait_send()
    final.wait()


def per_device(latents, steps, segment_ids, mod_table, w_query, w_key, w_value):
    anywhere = pl.BlockSpec(memory_space=pl.ANY)
    vmem = pltpu.VMEM
    dma = pltpu.SemaphoreType.DMA
    out = pl.pallas_call(
        kernel,
        out_shape=jax.ShapeDtypeStruct((2, 16, 4096), BF),
        in_specs=[anywhere, pl.BlockSpec(memory_space=pltpu.SMEM)] + [anywhere] * 5,
        out_specs=anywhere,
        scratch_shapes=[
            vmem((32, 16, D), BF),
            vmem((3, D, 256), BF),
            vmem((16, 2, D), F32),
            vmem((2, D), F32),
            vmem((128, D), BF),
            vmem((2, 32, 16, 3 * HD), BF),
            vmem((32, 16, 3 * HD), BF),
            vmem((16, 4, 16, HD), BF),
            vmem((16, 12, 16, 2 * HD), BF),
            vmem((256, 3072), F32),
            vmem((2, 256, 768), F32),
            vmem((1, 512), jnp.int32),
            vmem((16, 4, 16, HD), BF),
            vmem((2, 16, 4096), BF),
            dma((48,)),
            dma((33,)),
            dma((9,)),
            dma((16,)),
            dma((16,)),
            dma((2, 2, 8)),
            dma((2, 16)),
            dma((2, 2)),
            dma((2, 16)),
            dma((32,)),
        ],
        name="block",
        compiler_params=pltpu.CompilerParams(
            collective_id=0, has_side_effects=True, vmem_limit_bytes=58 * 1024 * 1024
        ),
    )(latents, steps, segment_ids.reshape(1, 512), mod_table, w_query, w_key, w_value)
    return out.reshape(1, 32, 4096)


def solution(mesh):
    placed = (
        P("group", "dp", None),
        P("group"),
        P(),
        P(),
        P(None, "dp"),
        P(None, "dp"),
        P(None, "dp"),
    )
    return jax.shard_map(
        per_device, mesh=mesh, in_specs=placed, out_specs=P("group", "dp", None), check_vma=False
    )
```

```python
import math

import jax
import jax.numpy as jnp
from jax import lax
from jax.experimental import pallas as pl
from jax.experimental.pallas import tpu as pltpu
from jax.sharding import PartitionSpec as P

D = 6144
HD = 128
HALF = D // 2
MESH = pl.DeviceIdType.MESH
NEG = -1e30
BF = jnp.bfloat16
F32 = jnp.float32


def kernel(
    lat, steps, seg, mod, wq, wk, wv, out,
    x_buf, w_buf, mod_all, mod_row, xn, own, partner, q_in, kv_in, s_buf, bias, seg_buf, o_buf, o_in,
    xs, xr, ls, ps, pr, es, er, lx, ds_, os_, or_,
):
    g = lax.axis_index("group")
    d = lax.axis_index("dp")
    xh = d // 8
    z = d % 8
    head = g // 8
    mate = (g + 8) % 16
    def window_of(place):
        core = place % 2
        return 4 * core + (place // 2 + z + 2 * core) % 4

    win = window_of(g % 8)

    def at_z(k):
        return {"group": g, "dp": xh * 8 + (z + k + 8) % 8}

    across = {"group": g, "dp": (d + 8) % 16}
    up, down = at_z(1), at_z(-1)

    barrier = pltpu.get_barrier_semaphore()
    for peer in (up, down, across):
        pl.semaphore_signal(barrier, inc=1, device_id=peer, device_id_type=MESH)
    for k in range(1, 16):
        pl.semaphore_signal(barrier, inc=1, device_id={"group": (g + k) % 16, "dp": d}, device_id_type=MESH)

    def block_same(k):
        return xh * 8 + (z + k + 8) % 8

    def block_other(k):
        return (1 - xh) * 8 + (z + k + 8) % 8

    def same(k, half):
        return 2 * block_same(k) + half

    def other(k, half):
        return 2 * block_other(k) + half

    loads = [
        pltpu.make_async_copy(lat.at[0, pl.ds(0, 16)], x_buf.at[same(0, 0)], ls.at[0]),
        pltpu.make_async_copy(lat.at[0, pl.ds(16, 16)], x_buf.at[same(0, 1)], ls.at[1]),
        pltpu.make_async_copy(mod, mod_all, ls.at[2]),
        pltpu.make_async_copy(seg, seg_buf, ls.at[3]),
        pltpu.make_async_copy(wq, w_buf.at[0], ls.at[4]),
        pltpu.make_async_copy(wk, w_buf.at[1], ls.at[5]),
        pltpu.make_async_copy(wv, w_buf.at[2], ls.at[6]),
    ]
    for c in loads:
        c.start()
    pl.semaphore_wait(barrier, 18)

    sends = []

    def send(src, dst, to, recv):
        c = pltpu.make_async_remote_copy(
            src_ref=src, dst_ref=dst, send_sem=xs.at[len(sends)], recv_sem=recv, device_id=to, device_id_type=MESH
        )
        c.start()
        sends.append(c)

    def send_own(half, to):
        send(lat.at[0, pl.ds(16 * half, 16)], x_buf.at[same(0, half)], to, xr.at[same(0, half)])

    def relay(slot, to):
        send(x_buf.at[slot], x_buf.at[slot], to, xr.at[slot])

    def relay_half(slot, part, to, second):
        cols = pl.ds(part * HALF, HALF)
        sem = xr.at[slot] if part == 0 else xr.at[second]
        send(x_buf.at[slot, :, cols], x_buf.at[slot, :, cols], to, sem)

    def arrived(slot):
        pltpu.make_async_remote_copy(
            src_ref=x_buf.at[slot], dst_ref=x_buf.at[slot], send_sem=xs.at[0], recv_sem=xr.at[slot],
            device_id=up, device_id_type=MESH,
        ).wait_recv()

    def arrived_half(slot, part, second):
        cols = pl.ds(part * HALF, HALF)
        sem = xr.at[slot] if part == 0 else xr.at[second]
        pltpu.make_async_remote_copy(
            src_ref=x_buf.at[slot, :, cols], dst_ref=x_buf.at[slot, :, cols], send_sem=xs.at[0], recv_sem=sem,
            device_id=up, device_id_type=MESH,
        ).wait_recv()

    send_own(0, across)
    send_own(1, up)
    send_own(1, down)
    send_own(0, up)
    send_own(0, down)
    send_own(1, across)

    loads[2].wait()
    row = mod_all[steps[0]]
    mod_row[0:1, :] = 1.0 + row[0:1, :]
    mod_row[1:2, :] = row[1:2, :]
    loads[3].wait()
    for w in range(8):
        first = min(max(64 * w - 64, 0), 320)

        @pl.when(win == w)
        def _(w=w, first=first):
            sq = jnp.broadcast_to(seg_buf[0:1, 64 * w : 64 * w + 64].astype(F32), (64, 64))
            diag = lax.broadcasted_iota(jnp.int32, (64, 64), 0) == lax.broadcasted_iota(jnp.int32, (64, 64), 1)
            col = jnp.sum(jnp.where(diag, sq, 0.0), axis=1, keepdims=True)
            sk = seg_buf[0:1, first : first + 192].astype(F32)
            tile = jnp.where(col == sk, 0.0, NEG)
            wide = jnp.concatenate([tile] * 4, axis=1)
            for i in range(4):
                bias[0, 64 * i : 64 * i + 64, :] = wide
                parts = [tile if j <= i else jnp.full((64, 192), NEG, F32) for j in range(4)]
                bias[1, 64 * i : 64 * i + 64, :] = jnp.concatenate(parts, axis=1)

    def norm(slot, at):
        x = x_buf[slot].astype(F32)
        inv = lax.rsqrt(jnp.mean(x * x, axis=-1, keepdims=True) + 1e-06)
        xn[pl.ds(16 * at, 16), :] = (x * inv * mod_row[0:1, :] + mod_row[1:2, :]).astype(BF)

    def project(which, slots):
        n = 16 * len(slots)
        r = jnp.dot(xn[0:n, :], w_buf[which], preferred_element_type=F32).astype(BF)
        for i, slot in enumerate(slots):
            for h in range(2):
                own[h, slot, :, HD * which : HD * which + HD] = r[16 * i : 16 * i + 16, HD * h : HD * h + HD]

    def swap(block):
        two = pl.ds(2 * block, 2)
        return pltpu.make_async_remote_copy(
            src_ref=own.at[1 - head, two], dst_ref=partner.at[two], send_sem=ps.at[block], recv_sem=pr.at[block],
            device_id={"group": mate, "dp": d}, device_id_type=MESH,
        )

    def place_of(w):
        return 2 * ((w % 4 + 2 * (w // 4) + 8 - z) % 4) + w // 4

    def reach(mid):
        low = jnp.where(mid == 2, 0, jnp.maximum(mid - 1, 0))
        high = jnp.where(mid == 5, 7, jnp.minimum(mid + 1, 7))
        return low, high + 1

    def rest_of(block, w):
        return pl.ds(2 * block - 4 * (jnp.minimum(jnp.maximum(w, 1), 6) - 1), 2)

    def spread(block, whose, keys=True, queries=True):
        src = own.at[head] if whose == 0 else partner
        c = g if whose == 0 else mate
        two = pl.ds(2 * block, 2)
        mid = block // 2
        kv_src = src.at[two, :, pl.ds(HD, 2 * HD)]

        def to_window(w, carry):
            place = place_of(w)
            here = place == g % 8
            kv_dst = kv_in.at[c, rest_of(block, w)]

            @pl.when(jnp.logical_not(here))
            def _():
                pltpu.make_async_remote_copy(
                    src_ref=kv_src, dst_ref=kv_dst, send_sem=es.at[0, whose, place], recv_sem=er.at[0, c],
                    device_id={"group": head * 8 + place, "dp": d}, device_id_type=MESH,
                ).start()

            @pl.when(here)
            def _():
                pltpu.make_async_copy(kv_src, kv_dst, lx.at[0, whose]).start()

            return carry

        if keys:
            lax.fori_loop(*reach(mid), to_window, 0)
        if queries:
            place = place_of(mid)
            here = place == g % 8
            q_src, q_dst = src.at[two, :, pl.ds(0, HD)], q_in.at[c, pl.ds(2 * (block % 2), 2)]

            @pl.when(jnp.logical_not(here))
            def _():
                pltpu.make_async_remote_copy(
                    src_ref=q_src, dst_ref=q_dst, send_sem=es.at[1, whose, place], recv_sem=er.at[1, c],
                    device_id={"group": head * 8 + place, "dp": d}, device_id_type=MESH,
                ).start()

            @pl.when(here)
            def _():
                pltpu.make_async_copy(q_src, q_dst, lx.at[1, whose]).start()

    def direct_keys(block, i, w):
        return pltpu.make_async_remote_copy(
            src_ref=own.at[1 - head, pl.ds(2 * block, 2), :, pl.ds(HD, 2 * HD)], dst_ref=kv_in.at[g, rest_of(block, w)],
            send_sem=ds_.at[i, w], recv_sem=er.at[0, g],
            device_id={"group": (1 - head) * 8 + place_of(w), "dp": d}, device_id_type=MESH,
        )

    def direct_queries(block, i):
        w = block // 2
        return pltpu.make_async_remote_copy(
            src_ref=own.at[1 - head, pl.ds(2 * block, 2), :, pl.ds(0, HD)],
            dst_ref=q_in.at[g, pl.ds(2 * (block % 2), 2)], send_sem=ds_.at[i, 8], recv_sem=er.at[1, g],
            device_id={"group": (1 - head) * 8 + place_of(w), "dp": d}, device_id_type=MESH,
        )

    def over_reach(block, call):
        def step(w, carry):
            call(w)
            return carry

        lax.fori_loop(*reach(block // 2), step, 0)

    todo = []

    def work(budget):
        while todo and budget > 0:
            cost, call = todo.pop(0)
            call()
            budget -= cost

    def norms(slots, at, wait):
        def call():
            for i in at:
                if wait:
                    arrived(slots[i])
                norm(slots[i], i)
        return call

    straight = [block_other(-3), block_other(3), block_same(4), block_other(4)]

    def out_keys(which):
        for i in which:
            over_reach(straight[i], lambda w, i=i: direct_keys(straight[i], i, w).start())
            spread(straight[i], 0, queries=False)

    def out_queries(which):
        for i in which:
            direct_queries(straight[i], i).start()
            spread(straight[i], 0, keys=False)

    def plan(slots, blocks, before, crossed=True):
        n = len(slots)
        for at in range(0, n, 2):
            wait = crossed and at == n - 2
            todo.append((0.5 if at < 4 else 1.0, norms(slots, (at, at + 1), wait)))
        for which in range(3):
            todo.append((1.0, lambda which=which: project(which, slots)))

        def out_own():
            for b in blocks:
                swap(b).start()
            for b in blocks:
                spread(b, 0)

        todo.append((1.0, out_own))
        if before:
            todo.append((0.5, lambda: out_mate(before)))

    def out_mate(blocks):
        for b in blocks:
            swap(b).wait_recv()
        for b in blocks:
            spread(b, 1)

    arrived(other(0, 0))
    relay(other(0, 0), up)
    relay(other(0, 0), down)
    loads[0].wait()
    loads[1].wait()
    slots = [same(0, 0), same(0, 1), other(0, 0), other(0, 1)]
    blocks = [block_same(0), block_other(0)]
    todo.append((0.5, norms(slots, (0, 1), False)))
    todo.append((0.5, norms(slots, (2,), False)))

    def ready():
        for i in (4, 5, 6):
            loads[i].wait()
        arrived(slots[3])
        norm(slots[3], 3)

    todo.append((0.5, lambda ready=ready: ready()))
    for which in range(3):
        todo.append((1.0, lambda which=which, slots=slots: project(which, slots)))

    def first_out(blocks=blocks):
        for b in blocks:
            swap(b).start()
        for b in blocks:
            spread(b, 0)

    todo.append((1.0, first_out))

    before = blocks
    for s in range(1, 4):
        a, b = same(-s, 1), same(s, 1)
        arrived(a)
        if s < 3:
            relay(a, up)
        relay(a, across)
        arrived(b)
        if s < 3:
            relay(b, down)
        else:
            relay_half(b, 0, down, 33)
            relay_half(b, 1, down, 33)
        relay(b, across)
        work(2.0)
        a, b = same(-s, 0), same(s, 0)
        arrived(a)
        relay(a, up)
        arrived(b)
        if s < 3:
            relay(b, down)
        if s < 3:
            work(2.0)
        else:
            work(100.0)
            chunk = [same(-s, 0), same(s, 0), same(-s, 1), same(s, 1)]
            blocks = [block_same(-s), block_same(s)]
            plan(chunk, blocks, before, crossed=False)
            before = blocks
            work(1.0)
        a, b = other(-s, 0), other(s, 0)
        arrived(a)
        if s < 3:
            relay(a, up)
        else:
            relay_half(a, 0, up, 32)
        arrived(b)
        if s < 3:
            relay(b, down)
            chunk = [same(-s, 0), same(s, 0), same(-s, 1), same(s, 1), other(-s, 0), other(s, 0), other(-s, 1), other(s, 1)]
            blocks = [block_same(-s), block_same(s), block_other(-s), block_other(s)]
        else:
            relay_half(b, 1, down, 32)
            chunk = [other(-s, 0), other(s, 0), other(-s, 1), other(s, 1)]
            blocks = [block_other(-s), block_other(s)]
        if s < 3:
            work(2.0)
            plan(chunk, blocks, before)
            before = blocks
        else:
            work(100.0)
            todo.append((0.5, norms(chunk, (0, 1), False)))
            todo.append((0.5, norms(chunk, (2, 3), True)))
            for which in (1, 2):
                todo.append((1.0, lambda which=which, chunk=chunk: project(which, chunk)))
            todo.append((0.5, lambda: out_keys((0, 1))))
            todo.append((1.0, lambda chunk=chunk: project(0, chunk)))
            todo.append((0.5, lambda: out_queries((0, 1))))

    def finish(slots, which):
        project(1, slots)
        project(2, slots)
        out_keys(which)
        project(0, slots)
        out_queries(which)

    mine, theirs = [same(4, 0), same(4, 1)], [other(4, 0), other(4, 1)]
    work(2.0)
    for part in range(2):
        arrived_half(mine[1], part, 33)
        relay_half(mine[1], part, across, 34)
        work(1.0)
    work(100.0)
    arrived(mine[0])
    norm(mine[0], 0)
    norm(mine[1], 1)
    finish(mine, (2,))
    out_mate(before)
    arrived_half(theirs[0], 0, 32)
    arrived_half(theirs[0], 1, 32)
    norm(theirs[0], 0)
    arrived_half(theirs[1], 0, 34)
    arrived_half(theirs[1], 1, 34)
    norm(theirs[1], 1)
    finish(theirs, (3,))

    def late(i, w):
        n = 0
        for b in straight:
            low, high = reach(b // 2)
            hit = jnp.logical_and(w >= low, w < high) if i == 0 else b // 2 == w
            n = n + jnp.where(hit, 1, 0)
        return n

    def units(i, n, c, send_sem, recv_sem):
        cols = pl.ds(HD, 2 * HD) if i == 0 else pl.ds(0, HD)
        return pltpu.make_async_remote_copy(
            src_ref=own.at[0, pl.ds(0, n), :, cols], dst_ref=(kv_in, q_in)[i].at[c, pl.ds(0, n)],
            send_sem=send_sem, recv_sem=recv_sem, device_id=up, device_id_type=MESH,
        )

    def local_units(i, n, c, sem):
        cols = pl.ds(HD, 2 * HD) if i == 0 else pl.ds(0, HD)
        return pltpu.make_async_copy(own.at[0, pl.ds(0, n), :, cols], (kv_in, q_in)[i].at[c, pl.ds(0, n)], sem)

    WHOLE = (12, 4)

    for i in range(2):
        local_units(i, WHOLE[i], g, lx.at[i, 0]).wait()
        n = late(i, win)
        for j in range(5):
            @pl.when(n == j)
            def _(i=i, j=j):
                if WHOLE[i] > 2 * j:
                    local_units(i, WHOLE[i] - 2 * j, mate, lx.at[i, 1]).wait()
                if 0 < 2 * j <= WHOLE[i]:
                    units(i, 2 * j, mate, es.at[i, 0, 0], er.at[i, mate]).wait_recv()
    for k in range(1, 8):
        c = (g + k) % 8
        for side in range(2):
            for i in range(2):
                units(i, WHOLE[i], c + 8 * side, es.at[i, 0, 0], er.at[i, c + 8 * side]).wait_recv()

    scale = math.log2(math.e) / math.sqrt(HD)

    def score(b):
        q = q_in[4 * b : 4 * b + 4].reshape(256, HD)
        best = jnp.full((256, 1), NEG, F32)
        for kb in range(b + 1):
            keys = kv_in[4 * kb : 4 * kb + 4, :, :, 0:HD].reshape(768, HD)
            sc = lax.dot_general(q, keys, (((1,), (1,)), ((), ())), preferred_element_type=F32)
            sc = sc * scale + bias[1 if kb == b else 0]
            s_buf[b % 2, :, 768 * kb : 768 * kb + 768] = sc
            best = jnp.maximum(best, jnp.max(sc, axis=-1, keepdims=True))
        return best

    def attend(b, best):
        total = jnp.zeros((256, 1), F32)
        acc = jnp.zeros((256, HD), F32)
        for kb in range(b + 1):
            p = jnp.exp2(s_buf[b % 2, :, 768 * kb : 768 * kb + 768] - best)
            total = total + jnp.sum(p, axis=-1, keepdims=True)
            vals = kv_in[4 * kb : 4 * kb + 4, :, :, HD : 2 * HD].reshape(768, HD)
            acc = acc + jnp.dot(p.astype(BF), vals, preferred_element_type=F32)
        o_buf[4 * b : 4 * b + 4] = (acc / total).astype(BF).reshape(4, 4, 16, HD)

    cols = pl.ds(pl.multiple_of((2 * d + head) * HD, HD), HD)

    def home(c, half):
        return pltpu.make_async_remote_copy(
            src_ref=o_buf.at[c, pl.ds(2 * half, 2)], dst_ref=o_in.at[:, :, cols], send_sem=os_.at[half, c],
            recv_sem=or_.at[2 * d + head], device_id={"group": c, "dp": 2 * win + half}, device_id_type=MESH,
        )

    def away(c, half):
        return jnp.logical_or(g != c, d != 2 * win + half)

    def send_home(b):
        for c in range(4 * b, 4 * b + 4):
            for half in range(2):
                far = away(c, half)

                @pl.when(far)
                def _(c=c, half=half):
                    home(c, half).start()

                @pl.when(jnp.logical_not(far))
                def _(c=c, half=half):
                    lc = pltpu.make_async_copy(o_buf.at[c, pl.ds(2 * half, 2)], o_in.at[:, :, cols], ls.at[7])
                    lc.start()
                    lc.wait()

    best = score(3)
    for b in (3, 2, 1, 0):
        attend(b, best)
        if b > 0:
            best = score(b - 1)
        send_home(b)

    for hd in range(32):
        src_d = hd // 2
        src_w = d // 2
        src_g = (hd % 2) * 8 + 2 * ((src_w % 4 + 2 * (src_w // 4) + 8 - src_d % 8) % 4) + src_w // 4
        remote = jnp.logical_or(src_g != g, src_d != d)

        @pl.when(remote)
        def _(hd=hd):
            pltpu.make_async_remote_copy(
                src_ref=o_buf.at[0, pl.ds(0, 2)], dst_ref=o_in.at[:, :, pl.ds(hd * HD, HD)], send_sem=os_.at[0, 0],
                recv_sem=or_.at[hd], device_id=up, device_id_type=MESH,
            ).wait_recv()

    final = pltpu.make_async_copy(o_in, out, ls.at[8])
    final.start()

    for c in sends:
        c.wait_send()
    for k in range(-3, 4):
        swap(block_same(k)).wait_send()
    for k in range(-2, 3):
        swap(block_other(k)).wait_send()
    for i, b in enumerate(straight):
        over_reach(b, lambda w, b=b, i=i: direct_keys(b, i, w).wait_send())
        direct_queries(b, i).wait_send()
    for k in range(1, 8):
        place = (g + k) % 8
        for i in range(2):
            units(i, WHOLE[i], 0, es.at[i, 0, place], er.at[i, 0]).wait_send()
            n = late(i, window_of(place))
            for j in range(5):
                if WHOLE[i] > 2 * j:
                    @pl.when(n == j)
                    def _(i=i, j=j, place=place):
                        units(i, WHOLE[i] - 2 * j, 0, es.at[i, 1, place], er.at[i, 0]).wait_send()
    for half in range(2):
        for c in range(16):
            @pl.when(away(c, half))
            def _(half=half, c=c):
                home(c, half).wait_send()
    final.wait()


def per_device(latents, steps, segment_ids, mod_table, w_query, w_key, w_value):
    anywhere = pl.BlockSpec(memory_space=pl.ANY)
    vmem = pltpu.VMEM
    dma = pltpu.SemaphoreType.DMA
    out = pl.pallas_call(
        kernel,
        out_shape=jax.ShapeDtypeStruct((2, 16, 4096), BF),
        in_specs=[anywhere, pl.BlockSpec(memory_space=pltpu.SMEM)] + [anywhere] * 5,
        out_specs=anywhere,
        scratch_shapes=[
            vmem((32, 16, D), BF),
            vmem((3, D, 256), BF),
            vmem((16, 2, D), F32),
            vmem((2, D), F32),
            vmem((128, D), BF),
            vmem((2, 32, 16, 3 * HD), BF),
            vmem((32, 16, 3 * HD), BF),
            vmem((16, 4, 16, HD), BF),
            vmem((16, 12, 16, 2 * HD), BF),
            vmem((2, 256, 3072), F32),
            vmem((2, 256, 768), F32),
            vmem((1, 512), jnp.int32),
            vmem((16, 4, 16, HD), BF),
            vmem((2, 16, 4096), BF),
            dma((48,)),
            dma((35,)),
            dma((9,)),
            dma((16,)),
            dma((16,)),
            dma((2, 2, 8)),
            dma((2, 16)),
            dma((2, 2)),
            dma((4, 9)),
            dma((2, 16)),
            dma((32,)),
        ],
        name="block",
        compiler_params=pltpu.CompilerParams(
            collective_id=0, has_side_effects=True, vmem_limit_bytes=58 * 1024 * 1024
        ),
    )(latents, steps, segment_ids.reshape(1, 512), mod_table, w_query, w_key, w_value)
    return out.reshape(1, 32, 4096)


def solution(mesh):
    placed = (
        P("group", "dp", None),
        P("group"),
        P(),
        P(),
        P(None, "dp"),
        P(None, "dp"),
        P(None, "dp"),
    )
    return jax.shard_map(
        per_device, mesh=mesh, in_specs=placed, out_specs=P("group", "dp", None), check_vma=False
    )
```

```python
import math

import jax
import jax.numpy as jnp
from jax import lax
from jax.experimental import pallas as pl
from jax.experimental.pallas import tpu as pltpu
from jax.sharding import PartitionSpec as P

D = 6144
HD = 128
HALF = D // 2
MESH = pl.DeviceIdType.MESH
NEG = -1e30
BF = jnp.bfloat16
F32 = jnp.float32


def kernel(
    lat, steps, seg, mod, wq, wk, wv, out,
    x_buf, w_buf, mod_all, mod_row, xn, own, partner, q_in, kv_in, s_buf, bias, seg_buf, o_buf, o_in,
    xs, xr, ls, ps, pr, es, er, lx, ds_, os_, or_,
):
    g = lax.axis_index("group")
    d = lax.axis_index("dp")
    xh = d // 8
    z = d % 8
    head = g // 8
    mate = (g + 8) % 16
    def window_of(place):
        core = place % 2
        return 4 * core + (place // 2 + z + 2 * core) % 4

    win = window_of(g % 8)

    def at_z(k):
        return {"group": g, "dp": xh * 8 + (z + k + 8) % 8}

    across = {"group": g, "dp": (d + 8) % 16}
    up, down = at_z(1), at_z(-1)

    barrier = pltpu.get_barrier_semaphore()
    for peer in (up, down, across):
        pl.semaphore_signal(barrier, inc=1, device_id=peer, device_id_type=MESH)
    for k in range(1, 16):
        pl.semaphore_signal(barrier, inc=1, device_id={"group": (g + k) % 16, "dp": d}, device_id_type=MESH)

    def block_same(k):
        return xh * 8 + (z + k + 8) % 8

    def block_other(k):
        return (1 - xh) * 8 + (z + k + 8) % 8

    def same(k, half):
        return 2 * block_same(k) + half

    def other(k, half):
        return 2 * block_other(k) + half

    loads = [
        pltpu.make_async_copy(lat.at[0, pl.ds(0, 16)], x_buf.at[same(0, 0)], ls.at[0]),
        pltpu.make_async_copy(lat.at[0, pl.ds(16, 16)], x_buf.at[same(0, 1)], ls.at[1]),
        pltpu.make_async_copy(mod, mod_all, ls.at[2]),
        pltpu.make_async_copy(seg, seg_buf, ls.at[3]),
        pltpu.make_async_copy(wq, w_buf.at[0], ls.at[4]),
        pltpu.make_async_copy(wk, w_buf.at[1], ls.at[5]),
        pltpu.make_async_copy(wv, w_buf.at[2], ls.at[6]),
    ]
    for c in loads:
        c.start()
    pl.semaphore_wait(barrier, 18)

    sends = []

    def send(src, dst, to, recv):
        c = pltpu.make_async_remote_copy(
            src_ref=src, dst_ref=dst, send_sem=xs.at[len(sends)], recv_sem=recv, device_id=to, device_id_type=MESH
        )
        c.start()
        sends.append(c)

    def send_own(half, to):
        send(lat.at[0, pl.ds(16 * half, 16)], x_buf.at[same(0, half)], to, xr.at[same(0, half)])

    def relay(slot, to):
        send(x_buf.at[slot], x_buf.at[slot], to, xr.at[slot])

    def relay_half(slot, part, to, second):
        cols = pl.ds(part * HALF, HALF)
        sem = xr.at[slot] if part == 0 else xr.at[second]
        send(x_buf.at[slot, :, cols], x_buf.at[slot, :, cols], to, sem)

    def arrived(slot):
        pltpu.make_async_remote_copy(
            src_ref=x_buf.at[slot], dst_ref=x_buf.at[slot], send_sem=xs.at[0], recv_sem=xr.at[slot],
            device_id=up, device_id_type=MESH,
        ).wait_recv()

    def arrived_half(slot, part, second):
        cols = pl.ds(part * HALF, HALF)
        sem = xr.at[slot] if part == 0 else xr.at[second]
        pltpu.make_async_remote_copy(
            src_ref=x_buf.at[slot, :, cols], dst_ref=x_buf.at[slot, :, cols], send_sem=xs.at[0], recv_sem=sem,
            device_id=up, device_id_type=MESH,
        ).wait_recv()

    send_own(0, across)
    send_own(1, up)
    send_own(1, down)
    send_own(0, up)
    send_own(0, down)
    send_own(1, across)

    loads[2].wait()
    row = mod_all[steps[0]]
    mod_row[0:1, :] = 1.0 + row[0:1, :]
    mod_row[1:2, :] = row[1:2, :]
    loads[3].wait()
    for w in range(8):
        first = min(max(64 * w - 64, 0), 320)

        @pl.when(win == w)
        def _(w=w, first=first):
            sq = jnp.broadcast_to(seg_buf[0:1, 64 * w : 64 * w + 64].astype(F32), (64, 64))
            diag = lax.broadcasted_iota(jnp.int32, (64, 64), 0) == lax.broadcasted_iota(jnp.int32, (64, 64), 1)
            col = jnp.sum(jnp.where(diag, sq, 0.0), axis=1, keepdims=True)
            sk = seg_buf[0:1, first : first + 192].astype(F32)
            tile = jnp.where(col == sk, 0.0, NEG)
            wide = jnp.concatenate([tile] * 4, axis=1)
            for i in range(4):
                bias[0, 64 * i : 64 * i + 64, :] = wide
                parts = [tile if j <= i else jnp.full((64, 192), NEG, F32) for j in range(4)]
                bias[1, 64 * i : 64 * i + 64, :] = jnp.concatenate(parts, axis=1)

    def norm(slot, at):
        x = x_buf[slot].astype(F32)
        inv = lax.rsqrt(jnp.mean(x * x, axis=-1, keepdims=True) + 1e-06)
        xn[pl.ds(16 * at, 16), :] = (x * inv * mod_row[0:1, :] + mod_row[1:2, :]).astype(BF)

    def project(which, slots):
        n = 16 * len(slots)
        r = jnp.dot(xn[0:n, :], w_buf[which], preferred_element_type=F32).astype(BF)
        for i, slot in enumerate(slots):
            for h in range(2):
                own[h, slot, :, HD * which : HD * which + HD] = r[16 * i : 16 * i + 16, HD * h : HD * h + HD]

    def swap(block):
        two = pl.ds(2 * block, 2)
        return pltpu.make_async_remote_copy(
            src_ref=own.at[1 - head, two], dst_ref=partner.at[two], send_sem=ps.at[block], recv_sem=pr.at[block],
            device_id={"group": mate, "dp": d}, device_id_type=MESH,
        )

    def place_of(w):
        return 2 * ((w % 4 + 2 * (w // 4) + 8 - z) % 4) + w // 4

    def reach(mid):
        low = jnp.where(mid == 2, 0, jnp.maximum(mid - 1, 0))
        high = jnp.where(mid == 5, 7, jnp.minimum(mid + 1, 7))
        return low, high + 1

    def rest_of(block, w):
        return pl.ds(2 * block - 4 * (jnp.minimum(jnp.maximum(w, 1), 6) - 1), 2)

    def spread(block, whose, keys=True, queries=True):
        src = own.at[head] if whose == 0 else partner
        c = g if whose == 0 else mate
        two = pl.ds(2 * block, 2)
        mid = block // 2
        kv_src = src.at[two, :, pl.ds(HD, 2 * HD)]

        def to_window(w, carry):
            place = place_of(w)
            here = place == g % 8
            kv_dst = kv_in.at[c, rest_of(block, w)]

            @pl.when(jnp.logical_not(here))
            def _():
                pltpu.make_async_remote_copy(
                    src_ref=kv_src, dst_ref=kv_dst, send_sem=es.at[0, whose, place], recv_sem=er.at[0, c],
                    device_id={"group": head * 8 + place, "dp": d}, device_id_type=MESH,
                ).start()

            @pl.when(here)
            def _():
                pltpu.make_async_copy(kv_src, kv_dst, lx.at[0, whose]).start()

            return carry

        if keys:
            lax.fori_loop(*reach(mid), to_window, 0)
        if queries:
            place = place_of(mid)
            here = place == g % 8
            q_src, q_dst = src.at[two, :, pl.ds(0, HD)], q_in.at[c, pl.ds(2 * (block % 2), 2)]

            @pl.when(jnp.logical_not(here))
            def _():
                pltpu.make_async_remote_copy(
                    src_ref=q_src, dst_ref=q_dst, send_sem=es.at[1, whose, place], recv_sem=er.at[1, c],
                    device_id={"group": head * 8 + place, "dp": d}, device_id_type=MESH,
                ).start()

            @pl.when(here)
            def _():
                pltpu.make_async_copy(q_src, q_dst, lx.at[1, whose]).start()

    def direct_keys(block, i, w):
        return pltpu.make_async_remote_copy(
            src_ref=own.at[1 - head, pl.ds(2 * block, 2), :, pl.ds(HD, 2 * HD)], dst_ref=kv_in.at[g, rest_of(block, w)],
            send_sem=ds_.at[i, w], recv_sem=er.at[0, g],
            device_id={"group": (1 - head) * 8 + place_of(w), "dp": d}, device_id_type=MESH,
        )

    def direct_queries(block, i):
        w = block // 2
        return pltpu.make_async_remote_copy(
            src_ref=own.at[1 - head, pl.ds(2 * block, 2), :, pl.ds(0, HD)],
            dst_ref=q_in.at[g, pl.ds(2 * (block % 2), 2)], send_sem=ds_.at[i, 8], recv_sem=er.at[1, g],
            device_id={"group": (1 - head) * 8 + place_of(w), "dp": d}, device_id_type=MESH,
        )

    def over_reach(block, call):
        def step(w, carry):
            call(w)
            return carry

        lax.fori_loop(*reach(block // 2), step, 0)

    todo = []

    def work(budget):
        while todo and budget > 0:
            cost, call = todo.pop(0)
            call()
            budget -= cost

    def norms(slots, at, wait):
        def call():
            for i in at:
                if wait:
                    arrived(slots[i])
                norm(slots[i], i)
        return call

    straight = [block_other(-3), block_other(3), block_same(4), block_other(4)]

    def out_keys(which):
        for i in which:
            over_reach(straight[i], lambda w, i=i: direct_keys(straight[i], i, w).start())
            spread(straight[i], 0, queries=False)

    def out_queries(which):
        for i in which:
            direct_queries(straight[i], i).start()
            spread(straight[i], 0, keys=False)

    def plan(slots, blocks, before, crossed=True):
        n = len(slots)
        for at in range(0, n, 2):
            wait = crossed and at == n - 2
            todo.append((0.5 if at < 4 else 1.0, norms(slots, (at, at + 1), wait)))
        for which in range(3):
            todo.append((1.0, lambda which=which: project(which, slots)))

        def out_own():
            for b in blocks:
                swap(b).start()
            for b in blocks:
                spread(b, 0)

        todo.append((1.0, out_own))
        if before:
            todo.append((0.5, lambda: out_mate(before)))

    def out_mate(blocks):
        for b in blocks:
            swap(b).wait_recv()
        for b in blocks:
            spread(b, 1)

    arrived(other(0, 0))
    relay(other(0, 0), up)
    relay(other(0, 0), down)
    loads[0].wait()
    loads[1].wait()
    slots = [same(0, 0), same(0, 1), other(0, 0), other(0, 1)]
    blocks = [block_same(0), block_other(0)]
    todo.append((0.5, norms(slots, (0, 1), False)))
    todo.append((0.5, norms(slots, (2,), False)))

    def ready():
        for i in (4, 5, 6):
            loads[i].wait()
        arrived(slots[3])
        norm(slots[3], 3)

    todo.append((0.5, lambda ready=ready: ready()))
    for which in range(3):
        todo.append((1.0, lambda which=which, slots=slots: project(which, slots)))

    def first_out(blocks=blocks):
        for b in blocks:
            swap(b).start()
        for b in blocks:
            spread(b, 0)

    todo.append((1.0, first_out))

    before = blocks
    for s in range(1, 4):
        a, b = same(-s, 1), same(s, 1)
        arrived(a)
        if s < 3:
            relay(a, up)
        relay(a, across)
        arrived(b)
        if s < 3:
            relay(b, down)
        else:
            relay(b, down)
        relay(b, across)
        work(2.0)
        a, b = same(-s, 0), same(s, 0)
        arrived(a)
        relay(a, up)
        arrived(b)
        if s < 3:
            relay(b, down)
        if s < 3:
            work(2.0)
        else:
            work(100.0)
            chunk = [same(-s, 0), same(s, 0), same(-s, 1), same(s, 1)]
            blocks = [block_same(-s), block_same(s)]
            plan(chunk, blocks, before, crossed=False)
            before = blocks
            work(1.0)
        a, b = other(-s, 0), other(s, 0)
        arrived(a)
        if s < 3:
            relay(a, up)
        else:
            relay_half(a, 0, up, 32)
        arrived(b)
        if s < 3:
            relay(b, down)
            chunk = [same(-s, 0), same(s, 0), same(-s, 1), same(s, 1), other(-s, 0), other(s, 0), other(-s, 1), other(s, 1)]
            blocks = [block_same(-s), block_same(s), block_other(-s), block_other(s)]
        else:
            relay_half(b, 1, down, 32)
            chunk = [other(-s, 0), other(s, 0), other(-s, 1), other(s, 1)]
            blocks = [block_other(-s), block_other(s)]
        if s < 3:
            work(2.0)
            plan(chunk, blocks, before)
            before = blocks
        else:
            work(100.0)
            todo.append((0.5, norms(chunk, (0, 1), False)))
            todo.append((0.5, norms(chunk, (2, 3), False)))
            for which in (1, 2):
                todo.append((1.0, lambda which=which, chunk=chunk: project(which, chunk)))
            todo.append((0.5, lambda: out_keys((0, 1))))
            todo.append((1.0, lambda chunk=chunk: project(0, chunk)))
            todo.append((0.5, lambda: out_queries((0, 1))))

    def finish(slots, which):
        project(1, slots)
        project(2, slots)
        out_keys(which)
        project(0, slots)
        out_queries(which)

    mine, theirs = [same(4, 0), same(4, 1)], [other(4, 0), other(4, 1)]
    arrived(other(-3, 1))
    relay_half(other(-3, 1), 0, up, 34)
    arrived(other(3, 1))
    relay_half(other(3, 1), 1, down, 34)
    work(100.0)
    arrived(mine[1])
    arrived(mine[0])
    norm(mine[0], 0)
    norm(mine[1], 1)
    finish(mine, (2,))
    out_mate(before)
    arrived_half(theirs[0], 0, 32)
    arrived_half(theirs[0], 1, 32)
    norm(theirs[0], 0)
    arrived_half(theirs[1], 0, 34)
    arrived_half(theirs[1], 1, 34)
    norm(theirs[1], 1)
    finish(theirs, (3,))

    def late(i, w):
        n = 0
        for b in straight:
            low, high = reach(b // 2)
            hit = jnp.logical_and(w >= low, w < high) if i == 0 else b // 2 == w
            n = n + jnp.where(hit, 1, 0)
        return n

    def units(i, n, c, send_sem, recv_sem):
        cols = pl.ds(HD, 2 * HD) if i == 0 else pl.ds(0, HD)
        return pltpu.make_async_remote_copy(
            src_ref=own.at[0, pl.ds(0, n), :, cols], dst_ref=(kv_in, q_in)[i].at[c, pl.ds(0, n)],
            send_sem=send_sem, recv_sem=recv_sem, device_id=up, device_id_type=MESH,
        )

    def local_units(i, n, c, sem):
        cols = pl.ds(HD, 2 * HD) if i == 0 else pl.ds(0, HD)
        return pltpu.make_async_copy(own.at[0, pl.ds(0, n), :, cols], (kv_in, q_in)[i].at[c, pl.ds(0, n)], sem)

    WHOLE = (12, 4)

    for i in range(2):
        local_units(i, WHOLE[i], g, lx.at[i, 0]).wait()
        n = late(i, win)
        for j in range(5):
            @pl.when(n == j)
            def _(i=i, j=j):
                if WHOLE[i] > 2 * j:
                    local_units(i, WHOLE[i] - 2 * j, mate, lx.at[i, 1]).wait()
                if 0 < 2 * j <= WHOLE[i]:
                    units(i, 2 * j, mate, es.at[i, 0, 0], er.at[i, mate]).wait_recv()
    for k in range(1, 8):
        c = (g + k) % 8
        for side in range(2):
            for i in range(2):
                units(i, WHOLE[i], c + 8 * side, es.at[i, 0, 0], er.at[i, c + 8 * side]).wait_recv()

    scale = math.log2(math.e) / math.sqrt(HD)

    def score(b):
        q = q_in[4 * b : 4 * b + 4].reshape(256, HD)
        best = jnp.full((256, 1), NEG, F32)
        for kb in range(b + 1):
            keys = kv_in[4 * kb : 4 * kb + 4, :, :, 0:HD].reshape(768, HD)
            sc = lax.dot_general(q, keys, (((1,), (1,)), ((), ())), preferred_element_type=F32)
            sc = sc * scale + bias[1 if kb == b else 0]
            s_buf[b % 2, :, 768 * kb : 768 * kb + 768] = sc
            best = jnp.maximum(best, jnp.max(sc, axis=-1, keepdims=True))
        return best

    def attend(b, best):
        total = jnp.zeros((256, 1), F32)
        acc = jnp.zeros((256, HD), F32)
        for kb in range(b + 1):
            p = jnp.exp2(s_buf[b % 2, :, 768 * kb : 768 * kb + 768] - best)
            total = total + jnp.sum(p, axis=-1, keepdims=True)
            vals = kv_in[4 * kb : 4 * kb + 4, :, :, HD : 2 * HD].reshape(768, HD)
            acc = acc + jnp.dot(p.astype(BF), vals, preferred_element_type=F32)
        o_buf[4 * b : 4 * b + 4] = (acc / total).astype(BF).reshape(4, 4, 16, HD)

    cols = pl.ds(pl.multiple_of((2 * d + head) * HD, HD), HD)

    def home(c, half):
        return pltpu.make_async_remote_copy(
            src_ref=o_buf.at[c, pl.ds(2 * half, 2)], dst_ref=o_in.at[:, :, cols], send_sem=os_.at[half, c],
            recv_sem=or_.at[2 * d + head], device_id={"group": c, "dp": 2 * win + half}, device_id_type=MESH,
        )

    def away(c, half):
        return jnp.logical_or(g != c, d != 2 * win + half)

    def send_home(b):
        for c in range(4 * b, 4 * b + 4):
            for half in range(2):
                far = away(c, half)

                @pl.when(far)
                def _(c=c, half=half):
                    home(c, half).start()

                @pl.when(jnp.logical_not(far))
                def _(c=c, half=half):
                    lc = pltpu.make_async_copy(o_buf.at[c, pl.ds(2 * half, 2)], o_in.at[:, :, cols], ls.at[7])
                    lc.start()
                    lc.wait()

    best = score(3)
    for b in (3, 2, 1, 0):
        attend(b, best)
        if b > 0:
            best = score(b - 1)
        send_home(b)

    for hd in range(32):
        src_d = hd // 2
        src_w = d // 2
        src_g = (hd % 2) * 8 + 2 * ((src_w % 4 + 2 * (src_w // 4) + 8 - src_d % 8) % 4) + src_w // 4
        remote = jnp.logical_or(src_g != g, src_d != d)

        @pl.when(remote)
        def _(hd=hd):
            pltpu.make_async_remote_copy(
                src_ref=o_buf.at[0, pl.ds(0, 2)], dst_ref=o_in.at[:, :, pl.ds(hd * HD, HD)], send_sem=os_.at[0, 0],
                recv_sem=or_.at[hd], device_id=up, device_id_type=MESH,
            ).wait_recv()

    final = pltpu.make_async_copy(o_in, out, ls.at[8])
    final.start()

    for c in sends:
        c.wait_send()
    for k in range(-3, 4):
        swap(block_same(k)).wait_send()
    for k in range(-2, 3):
        swap(block_other(k)).wait_send()
    for i, b in enumerate(straight):
        over_reach(b, lambda w, b=b, i=i: direct_keys(b, i, w).wait_send())
        direct_queries(b, i).wait_send()
    for k in range(1, 8):
        place = (g + k) % 8
        for i in range(2):
            units(i, WHOLE[i], 0, es.at[i, 0, place], er.at[i, 0]).wait_send()
            n = late(i, window_of(place))
            for j in range(5):
                if WHOLE[i] > 2 * j:
                    @pl.when(n == j)
                    def _(i=i, j=j, place=place):
                        units(i, WHOLE[i] - 2 * j, 0, es.at[i, 1, place], er.at[i, 0]).wait_send()
    for half in range(2):
        for c in range(16):
            @pl.when(away(c, half))
            def _(half=half, c=c):
                home(c, half).wait_send()
    final.wait()


def per_device(latents, steps, segment_ids, mod_table, w_query, w_key, w_value):
    anywhere = pl.BlockSpec(memory_space=pl.ANY)
    vmem = pltpu.VMEM
    dma = pltpu.SemaphoreType.DMA
    out = pl.pallas_call(
        kernel,
        out_shape=jax.ShapeDtypeStruct((2, 16, 4096), BF),
        in_specs=[anywhere, pl.BlockSpec(memory_space=pltpu.SMEM)] + [anywhere] * 5,
        out_specs=anywhere,
        scratch_shapes=[
            vmem((32, 16, D), BF),
            vmem((3, D, 256), BF),
            vmem((16, 2, D), F32),
            vmem((2, D), F32),
            vmem((128, D), BF),
            vmem((2, 32, 16, 3 * HD), BF),
            vmem((32, 16, 3 * HD), BF),
            vmem((16, 4, 16, HD), BF),
            vmem((16, 12, 16, 2 * HD), BF),
            vmem((2, 256, 3072), F32),
            vmem((2, 256, 768), F32),
            vmem((1, 512), jnp.int32),
            vmem((16, 4, 16, HD), BF),
            vmem((2, 16, 4096), BF),
            dma((48,)),
            dma((35,)),
            dma((9,)),
            dma((16,)),
            dma((16,)),
            dma((2, 2, 8)),
            dma((2, 16)),
            dma((2, 2)),
            dma((4, 9)),
            dma((2, 16)),
            dma((32,)),
        ],
        name="block",
        compiler_params=pltpu.CompilerParams(
            collective_id=0, has_side_effects=True, vmem_limit_bytes=58 * 1024 * 1024
        ),
    )(latents, steps, segment_ids.reshape(1, 512), mod_table, w_query, w_key, w_value)
    return out.reshape(1, 32, 4096)


def solution(mesh):
    placed = (
        P("group", "dp", None),
        P("group"),
        P(),
        P(),
        P(None, "dp"),
        P(None, "dp"),
        P(None, "dp"),
    )
    return jax.shard_map(
        per_device, mesh=mesh, in_specs=placed, out_specs=P("group", "dp", None), check_vma=False
    )
```

```python
import math

import jax
import jax.numpy as jnp
from jax import lax
from jax.experimental import pallas as pl
from jax.experimental.pallas import tpu as pltpu
from jax.sharding import PartitionSpec as P

D = 6144
HD = 128
HALF = D // 2
MESH = pl.DeviceIdType.MESH
NEG = -1e30
BF = jnp.bfloat16
F32 = jnp.float32


def kernel(
    lat, steps, seg, mod, wq, wk, wv, out,
    x_buf, w_buf, mod_all, mod_row, xn, own, partner, q_in, kv_in, s_buf, bias, seg_buf, o_buf, o_in,
    xs, xr, ls, ps, pr, es, er, lx, ds_, os_, or_,
):
    g = lax.axis_index("group")
    d = lax.axis_index("dp")
    xh = d // 8
    z = d % 8
    head = g // 8
    mate = (g + 8) % 16
    def window_of(place):
        core = place % 2
        return 4 * core + (place // 2 + z + 2 * core) % 4

    win = window_of(g % 8)

    def at_z(k):
        return {"group": g, "dp": xh * 8 + (z + k + 8) % 8}

    across = {"group": g, "dp": (d + 8) % 16}
    up, down = at_z(1), at_z(-1)

    barrier = pltpu.get_barrier_semaphore()
    for peer in (up, down, across):
        pl.semaphore_signal(barrier, inc=1, device_id=peer, device_id_type=MESH)
    for k in range(1, 16):
        pl.semaphore_signal(barrier, inc=1, device_id={"group": (g + k) % 16, "dp": d}, device_id_type=MESH)

    def block_same(k):
        return xh * 8 + (z + k + 8) % 8

    def block_other(k):
        return (1 - xh) * 8 + (z + k + 8) % 8

    def same(k, half):
        return 2 * block_same(k) + half

    def other(k, half):
        return 2 * block_other(k) + half

    loads = [
        pltpu.make_async_copy(lat.at[0, pl.ds(0, 16)], x_buf.at[same(0, 0)], ls.at[0]),
        pltpu.make_async_copy(lat.at[0, pl.ds(16, 16)], x_buf.at[same(0, 1)], ls.at[1]),
        pltpu.make_async_copy(mod, mod_all, ls.at[2]),
        pltpu.make_async_copy(seg, seg_buf, ls.at[3]),
        pltpu.make_async_copy(wq, w_buf.at[0], ls.at[4]),
        pltpu.make_async_copy(wk, w_buf.at[1], ls.at[5]),
        pltpu.make_async_copy(wv, w_buf.at[2], ls.at[6]),
    ]
    for c in loads:
        c.start()
    pl.semaphore_wait(barrier, 18)

    sends = []

    def send(src, dst, to, recv):
        c = pltpu.make_async_remote_copy(
            src_ref=src, dst_ref=dst, send_sem=xs.at[len(sends)], recv_sem=recv, device_id=to, device_id_type=MESH
        )
        c.start()
        sends.append(c)

    def send_own(half, to):
        send(lat.at[0, pl.ds(16 * half, 16)], x_buf.at[same(0, half)], to, xr.at[same(0, half)])

    def relay(slot, to):
        send(x_buf.at[slot], x_buf.at[slot], to, xr.at[slot])

    def relay_half(slot, part, to, second):
        cols = pl.ds(part * HALF, HALF)
        sem = xr.at[slot] if part == 0 else xr.at[second]
        send(x_buf.at[slot, :, cols], x_buf.at[slot, :, cols], to, sem)

    def arrived(slot):
        pltpu.make_async_remote_copy(
            src_ref=x_buf.at[slot], dst_ref=x_buf.at[slot], send_sem=xs.at[0], recv_sem=xr.at[slot],
            device_id=up, device_id_type=MESH,
        ).wait_recv()

    def arrived_half(slot, part, second):
        cols = pl.ds(part * HALF, HALF)
        sem = xr.at[slot] if part == 0 else xr.at[second]
        pltpu.make_async_remote_copy(
            src_ref=x_buf.at[slot, :, cols], dst_ref=x_buf.at[slot, :, cols], send_sem=xs.at[0], recv_sem=sem,
            device_id=up, device_id_type=MESH,
        ).wait_recv()

    send_own(0, across)
    send_own(1, up)
    send_own(1, down)
    send_own(0, up)
    send_own(0, down)
    send_own(1, across)

    loads[2].wait()
    row = mod_all[steps[0]]
    mod_row[0:1, :] = 1.0 + row[0:1, :]
    mod_row[1:2, :] = row[1:2, :]
    loads[3].wait()
    for w in range(8):
        first = min(max(64 * w - 64, 0), 320)

        @pl.when(win == w)
        def _(w=w, first=first):
            sq = jnp.broadcast_to(seg_buf[0:1, 64 * w : 64 * w + 64].astype(F32), (64, 64))
            diag = lax.broadcasted_iota(jnp.int32, (64, 64), 0) == lax.broadcasted_iota(jnp.int32, (64, 64), 1)
            col = jnp.sum(jnp.where(diag, sq, 0.0), axis=1, keepdims=True)
            sk = seg_buf[0:1, first : first + 192].astype(F32)
            tile = jnp.where(col == sk, 0.0, NEG)
            wide = jnp.concatenate([tile] * 4, axis=1)
            for i in range(4):
                bias[0, 64 * i : 64 * i + 64, :] = wide
                parts = [tile if j <= i else jnp.full((64, 192), NEG, F32) for j in range(4)]
                bias[1, 64 * i : 64 * i + 64, :] = jnp.concatenate(parts, axis=1)

    def norm(slot, at):
        x = x_buf[slot].astype(F32)
        inv = lax.rsqrt(jnp.mean(x * x, axis=-1, keepdims=True) + 1e-06)
        xn[pl.ds(16 * at, 16), :] = (x * inv * mod_row[0:1, :] + mod_row[1:2, :]).astype(BF)

    def project(which, slots):
        n = 16 * len(slots)
        r = jnp.dot(xn[0:n, :], w_buf[which], preferred_element_type=F32).astype(BF)
        for i, slot in enumerate(slots):
            for h in range(2):
                own[h, slot, :, HD * which : HD * which + HD] = r[16 * i : 16 * i + 16, HD * h : HD * h + HD]

    def swap(block):
        two = pl.ds(2 * block, 2)
        return pltpu.make_async_remote_copy(
            src_ref=own.at[1 - head, two], dst_ref=partner.at[two], send_sem=ps.at[block], recv_sem=pr.at[block],
            device_id={"group": mate, "dp": d}, device_id_type=MESH,
        )

    def place_of(w):
        return 2 * ((w % 4 + 2 * (w // 4) + 8 - z) % 4) + w // 4

    def reach(mid):
        low = jnp.where(mid == 2, 0, jnp.maximum(mid - 1, 0))
        high = jnp.where(mid == 5, 7, jnp.minimum(mid + 1, 7))
        return low, high + 1

    def rest_of(block, w):
        return pl.ds(2 * block - 4 * (jnp.minimum(jnp.maximum(w, 1), 6) - 1), 2)

    def spread(block, whose, keys=True, queries=True):
        src = own.at[head] if whose == 0 else partner
        c = g if whose == 0 else mate
        two = pl.ds(2 * block, 2)
        mid = block // 2
        kv_src = src.at[two, :, pl.ds(HD, 2 * HD)]

        def to_window(w, carry):
            place = place_of(w)
            here = place == g % 8
            kv_dst = kv_in.at[c, rest_of(block, w)]

            @pl.when(jnp.logical_not(here))
            def _():
                pltpu.make_async_remote_copy(
                    src_ref=kv_src, dst_ref=kv_dst, send_sem=es.at[0, whose, place], recv_sem=er.at[0, c],
                    device_id={"group": head * 8 + place, "dp": d}, device_id_type=MESH,
                ).start()

            @pl.when(here)
            def _():
                pltpu.make_async_copy(kv_src, kv_dst, lx.at[0, whose]).start()

            return carry

        if keys:
            lax.fori_loop(*reach(mid), to_window, 0)
        if queries:
            place = place_of(mid)
            here = place == g % 8
            q_src, q_dst = src.at[two, :, pl.ds(0, HD)], q_in.at[c, pl.ds(2 * (block % 2), 2)]

            @pl.when(jnp.logical_not(here))
            def _():
                pltpu.make_async_remote_copy(
                    src_ref=q_src, dst_ref=q_dst, send_sem=es.at[1, whose, place], recv_sem=er.at[1, c],
                    device_id={"group": head * 8 + place, "dp": d}, device_id_type=MESH,
                ).start()

            @pl.when(here)
            def _():
                pltpu.make_async_copy(q_src, q_dst, lx.at[1, whose]).start()

    def direct_keys(block, i, w):
        return pltpu.make_async_remote_copy(
            src_ref=own.at[1 - head, pl.ds(2 * block, 2), :, pl.ds(HD, 2 * HD)], dst_ref=kv_in.at[g, rest_of(block, w)],
            send_sem=ds_.at[i, w], recv_sem=er.at[0, g],
            device_id={"group": (1 - head) * 8 + place_of(w), "dp": d}, device_id_type=MESH,
        )

    def direct_queries(block, i):
        w = block // 2
        return pltpu.make_async_remote_copy(
            src_ref=own.at[1 - head, pl.ds(2 * block, 2), :, pl.ds(0, HD)],
            dst_ref=q_in.at[g, pl.ds(2 * (block % 2), 2)], send_sem=ds_.at[i, 8], recv_sem=er.at[1, g],
            device_id={"group": (1 - head) * 8 + place_of(w), "dp": d}, device_id_type=MESH,
        )

    def over_reach(block, call):
        def step(w, carry):
            call(w)
            return carry

        lax.fori_loop(*reach(block // 2), step, 0)

    todo = []

    def work(budget):
        while todo and budget > 0:
            cost, call = todo.pop(0)
            call()
            budget -= cost

    def norms(slots, at, wait):
        def call():
            for i in at:
                if wait:
                    arrived(slots[i])
                norm(slots[i], i)
        return call

    straight = [block_other(-3), block_other(3), block_same(4), block_other(4), block_same(-3), block_same(3)]

    def out_keys(which):
        for i in which:
            over_reach(straight[i], lambda w, i=i: direct_keys(straight[i], i, w).start())
            spread(straight[i], 0, queries=False)

    def out_queries(which):
        for i in which:
            direct_queries(straight[i], i).start()
            spread(straight[i], 0, keys=False)

    def plan(slots, blocks, before):
        n = len(slots)
        for at in range(0, n, 2):
            wait = at == n - 2
            todo.append((0.5 if at < 4 else 1.0, norms(slots, (at, at + 1), wait)))
        for which in range(3):
            todo.append((1.0, lambda which=which: project(which, slots)))

        def out_own():
            for b in blocks:
                swap(b).start()
            for b in blocks:
                spread(b, 0)

        todo.append((1.0, out_own))
        if before:
            todo.append((0.5, lambda: out_mate(before)))

    def out_mate(blocks):
        for b in blocks:
            swap(b).wait_recv()
        for b in blocks:
            spread(b, 1)

    arrived(other(0, 0))
    relay(other(0, 0), up)
    relay(other(0, 0), down)
    loads[0].wait()
    loads[1].wait()
    slots = [same(0, 0), same(0, 1), other(0, 0), other(0, 1)]
    blocks = [block_same(0), block_other(0)]
    todo.append((0.5, norms(slots, (0, 1), False)))
    todo.append((0.5, norms(slots, (2,), False)))

    def ready():
        for i in (4, 5, 6):
            loads[i].wait()
        arrived(slots[3])
        norm(slots[3], 3)

    todo.append((0.5, lambda ready=ready: ready()))
    for which in range(3):
        todo.append((1.0, lambda which=which, slots=slots: project(which, slots)))

    def first_out(blocks=blocks):
        for b in blocks:
            swap(b).start()
        for b in blocks:
            spread(b, 0)

    todo.append((1.0, first_out))

    before = blocks
    for s in range(1, 4):
        a, b = same(-s, 1), same(s, 1)
        arrived(a)
        if s < 3:
            relay(a, up)
        relay(a, across)
        arrived(b)
        if s < 3:
            relay(b, down)
        else:
            relay(b, down)
        relay(b, across)
        work(2.0)
        a, b = same(-s, 0), same(s, 0)
        arrived(a)
        relay(a, up)
        arrived(b)
        if s < 3:
            relay(b, down)
        if s < 3:
            work(2.0)
        else:
            work(100.0)
            chunk = [same(-s, 0), same(s, 0), same(-s, 1), same(s, 1)]
            todo.append((0.5, norms(chunk, (0, 1), False)))
            todo.append((0.5, norms(chunk, (2, 3), False)))
            for which in (1, 2):
                todo.append((1.0, lambda which=which, chunk=chunk: project(which, chunk)))
            todo.append((0.5, lambda: out_keys((4, 5))))
            todo.append((1.0, lambda chunk=chunk: project(0, chunk)))
            todo.append((0.5, lambda: out_queries((4, 5))))
            todo.append((0.5, lambda before=before: out_mate(before)))
            work(1.0)
        a, b = other(-s, 0), other(s, 0)
        arrived(a)
        if s < 3:
            relay(a, up)
        else:
            relay_half(a, 0, up, 32)
        arrived(b)
        if s < 3:
            relay(b, down)
            chunk = [same(-s, 0), same(s, 0), same(-s, 1), same(s, 1), other(-s, 0), other(s, 0), other(-s, 1), other(s, 1)]
            blocks = [block_same(-s), block_same(s), block_other(-s), block_other(s)]
        else:
            relay_half(b, 1, down, 32)
            chunk = [other(-s, 0), other(s, 0), other(-s, 1), other(s, 1)]
            blocks = [block_other(-s), block_other(s)]
        if s < 3:
            work(2.0)
            plan(chunk, blocks, before)
            before = blocks
        else:
            work(100.0)
            todo.append((0.5, norms(chunk, (0, 1), False)))
            todo.append((0.5, norms(chunk, (2, 3), False)))
            for which in (1, 2):
                todo.append((1.0, lambda which=which, chunk=chunk: project(which, chunk)))
            todo.append((0.5, lambda: out_keys((0, 1))))
            todo.append((1.0, lambda chunk=chunk: project(0, chunk)))
            todo.append((0.5, lambda: out_queries((0, 1))))

    def finish(slots, which):
        project(1, slots)
        project(2, slots)
        out_keys(which)
        project(0, slots)
        out_queries(which)

    mine, theirs = [same(4, 0), same(4, 1)], [other(4, 0), other(4, 1)]
    arrived(other(-3, 1))
    relay_half(other(-3, 1), 0, up, 34)
    arrived(other(3, 1))
    relay_half(other(3, 1), 1, down, 34)
    work(100.0)
    arrived(mine[1])
    arrived(mine[0])
    norm(mine[0], 0)
    norm(mine[1], 1)
    finish(mine, (2,))
    arrived_half(theirs[0], 0, 32)
    arrived_half(theirs[0], 1, 32)
    norm(theirs[0], 0)
    arrived_half(theirs[1], 0, 34)
    arrived_half(theirs[1], 1, 34)
    norm(theirs[1], 1)
    finish(theirs, (3,))

    def late(i, w):
        n = 0
        for b in straight:
            low, high = reach(b // 2)
            hit = jnp.logical_and(w >= low, w < high) if i == 0 else b // 2 == w
            n = n + jnp.where(hit, 1, 0)
        return n

    def units(i, n, c, send_sem, recv_sem):
        cols = pl.ds(HD, 2 * HD) if i == 0 else pl.ds(0, HD)
        return pltpu.make_async_remote_copy(
            src_ref=own.at[0, pl.ds(0, n), :, cols], dst_ref=(kv_in, q_in)[i].at[c, pl.ds(0, n)],
            send_sem=send_sem, recv_sem=recv_sem, device_id=up, device_id_type=MESH,
        )

    def local_units(i, n, c, sem):
        cols = pl.ds(HD, 2 * HD) if i == 0 else pl.ds(0, HD)
        return pltpu.make_async_copy(own.at[0, pl.ds(0, n), :, cols], (kv_in, q_in)[i].at[c, pl.ds(0, n)], sem)

    WHOLE = (12, 4)

    for i in range(2):
        local_units(i, WHOLE[i], g, lx.at[i, 0]).wait()
        n = late(i, win)
        for j in range(7):
            @pl.when(n == j)
            def _(i=i, j=j):
                if WHOLE[i] > 2 * j:
                    local_units(i, WHOLE[i] - 2 * j, mate, lx.at[i, 1]).wait()
                if 0 < 2 * j <= WHOLE[i]:
                    units(i, 2 * j, mate, es.at[i, 0, 0], er.at[i, mate]).wait_recv()
    for k in range(1, 8):
        c = (g + k) % 8
        for side in range(2):
            for i in range(2):
                units(i, WHOLE[i], c + 8 * side, es.at[i, 0, 0], er.at[i, c + 8 * side]).wait_recv()

    scale = math.log2(math.e) / math.sqrt(HD)

    def score(b):
        q = q_in[4 * b : 4 * b + 4].reshape(256, HD)
        best = jnp.full((256, 1), NEG, F32)
        for kb in range(b + 1):
            keys = kv_in[4 * kb : 4 * kb + 4, :, :, 0:HD].reshape(768, HD)
            sc = lax.dot_general(q, keys, (((1,), (1,)), ((), ())), preferred_element_type=F32)
            sc = sc * scale + bias[1 if kb == b else 0]
            s_buf[b % 2, :, 768 * kb : 768 * kb + 768] = sc
            best = jnp.maximum(best, jnp.max(sc, axis=-1, keepdims=True))
        return best

    def attend(b, best):
        total = jnp.zeros((256, 1), F32)
        acc = jnp.zeros((256, HD), F32)
        for kb in range(b + 1):
            p = jnp.exp2(s_buf[b % 2, :, 768 * kb : 768 * kb + 768] - best)
            total = total + jnp.sum(p, axis=-1, keepdims=True)
            vals = kv_in[4 * kb : 4 * kb + 4, :, :, HD : 2 * HD].reshape(768, HD)
            acc = acc + jnp.dot(p.astype(BF), vals, preferred_element_type=F32)
        o_buf[4 * b : 4 * b + 4] = (acc / total).astype(BF).reshape(4, 4, 16, HD)

    cols = pl.ds(pl.multiple_of((2 * d + head) * HD, HD), HD)

    def home(c, half):
        return pltpu.make_async_remote_copy(
            src_ref=o_buf.at[c, pl.ds(2 * half, 2)], dst_ref=o_in.at[:, :, cols], send_sem=os_.at[half, c],
            recv_sem=or_.at[2 * d + head], device_id={"group": c, "dp": 2 * win + half}, device_id_type=MESH,
        )

    def away(c, half):
        return jnp.logical_or(g != c, d != 2 * win + half)

    def send_home(b):
        for c in range(4 * b, 4 * b + 4):
            for half in range(2):
                far = away(c, half)

                @pl.when(far)
                def _(c=c, half=half):
                    home(c, half).start()

                @pl.when(jnp.logical_not(far))
                def _(c=c, half=half):
                    lc = pltpu.make_async_copy(o_buf.at[c, pl.ds(2 * half, 2)], o_in.at[:, :, cols], ls.at[7])
                    lc.start()
                    lc.wait()

    best = score(3)
    for b in (3, 2, 1, 0):
        attend(b, best)
        if b > 0:
            best = score(b - 1)
        send_home(b)

    for hd in range(32):
        src_d = hd // 2
        src_w = d // 2
        src_g = (hd % 2) * 8 + 2 * ((src_w % 4 + 2 * (src_w // 4) + 8 - src_d % 8) % 4) + src_w // 4
        remote = jnp.logical_or(src_g != g, src_d != d)

        @pl.when(remote)
        def _(hd=hd):
            pltpu.make_async_remote_copy(
                src_ref=o_buf.at[0, pl.ds(0, 2)], dst_ref=o_in.at[:, :, pl.ds(hd * HD, HD)], send_sem=os_.at[0, 0],
                recv_sem=or_.at[hd], device_id=up, device_id_type=MESH,
            ).wait_recv()

    final = pltpu.make_async_copy(o_in, out, ls.at[8])
    final.start()

    for c in sends:
        c.wait_send()
    for k in range(-2, 3):
        swap(block_same(k)).wait_send()
        swap(block_other(k)).wait_send()
    for i, b in enumerate(straight):
        over_reach(b, lambda w, b=b, i=i: direct_keys(b, i, w).wait_send())
        direct_queries(b, i).wait_send()
    for k in range(1, 8):
        place = (g + k) % 8
        for i in range(2):
            units(i, WHOLE[i], 0, es.at[i, 0, place], er.at[i, 0]).wait_send()
            n = late(i, window_of(place))
            for j in range(7):
                if WHOLE[i] > 2 * j:
                    @pl.when(n == j)
                    def _(i=i, j=j, place=place):
                        units(i, WHOLE[i] - 2 * j, 0, es.at[i, 1, place], er.at[i, 0]).wait_send()
    for half in range(2):
        for c in range(16):
            @pl.when(away(c, half))
            def _(half=half, c=c):
                home(c, half).wait_send()
    final.wait()


def per_device(latents, steps, segment_ids, mod_table, w_query, w_key, w_value):
    anywhere = pl.BlockSpec(memory_space=pl.ANY)
    vmem = pltpu.VMEM
    dma = pltpu.SemaphoreType.DMA
    out = pl.pallas_call(
        kernel,
        out_shape=jax.ShapeDtypeStruct((2, 16, 4096), BF),
        in_specs=[anywhere, pl.BlockSpec(memory_space=pltpu.SMEM)] + [anywhere] * 5,
        out_specs=anywhere,
        scratch_shapes=[
            vmem((32, 16, D), BF),
            vmem((3, D, 256), BF),
            vmem((16, 2, D), F32),
            vmem((2, D), F32),
            vmem((128, D), BF),
            vmem((2, 32, 16, 3 * HD), BF),
            vmem((32, 16, 3 * HD), BF),
            vmem((16, 4, 16, HD), BF),
            vmem((16, 12, 16, 2 * HD), BF),
            vmem((2, 256, 3072), F32),
            vmem((2, 256, 768), F32),
            vmem((1, 512), jnp.int32),
            vmem((16, 4, 16, HD), BF),
            vmem((2, 16, 4096), BF),
            dma((48,)),
            dma((35,)),
            dma((9,)),
            dma((16,)),
            dma((16,)),
            dma((2, 2, 8)),
            dma((2, 16)),
            dma((2, 2)),
            dma((6, 9)),
            dma((2, 16)),
            dma((32,)),
        ],
        name="block",
        compiler_params=pltpu.CompilerParams(
            collective_id=0, has_side_effects=True, vmem_limit_bytes=58 * 1024 * 1024
        ),
    )(latents, steps, segment_ids.reshape(1, 512), mod_table, w_query, w_key, w_value)
    return out.reshape(1, 32, 4096)


def solution(mesh):
    placed = (
        P("group", "dp", None),
        P("group"),
        P(),
        P(),
        P(None, "dp"),
        P(None, "dp"),
        P(None, "dp"),
    )
    return jax.shard_map(
        per_device, mesh=mesh, in_specs=placed, out_specs=P("group", "dp", None), check_vma=False
    )
```
